32 devices in a mesh: grp: 2 (over x), row: 8 (over z, y), col: 2 (over core).
Axes of the slice: x: 2, y: 2, z: 4, core: 2. Of those that a mesh axis runs over, the one named last changes fastest.
Arguments:
- query_window: bfloat16 [16, 8, 128, 1280], P(('grp', 'row'), 'col'), parts along dimension 0, may hold values from -80 to 80
- key_window: bfloat16 [16, 8, 128, 1280], P(('grp', 'row'), 'col'), parts along dimension 0, may hold values from -9 to 9
- value_window: bfloat16 [16, 8, 128, 1280], P(('grp', 'row'), 'col'), parts along dimension 0, may hold values from -6 to 6
- query_index: bfloat16 [16, 8, 128, 1280], P(('grp', 'row'), 'col'), parts along dimension 0, may hold values from -80 to 80
- key_index: bfloat16 [16, 8, 128, 1280], P(('grp', 'row'), 'col'), parts along dimension 0, may hold values from -9 to 9
- proj_weight: bfloat16 [1280, 1024], replicated, may hold values from -0.5 to 0.5
- proj_bias: float32 [1024], replicated, may hold values from -3 to 3
- first_kernel: bfloat16 [3, 3, 256, 256], replicated, may hold values from -0.125 to 0.125
- first_bias: float32 [256], replicated, may hold values from -3 to 3
- second_kernel: bfloat16 [3, 3, 256, 256], replicated, may hold values from -0.125 to 0.125
- second_bias: float32 [256], replicated, may hold values from -3 to 3
Outputs:
- fine_field: bfloat16 [256, 256, 256], P(('grp', 'row'), 'col'), parts along dimension 0
The draws below stay inside these ranges and needn't reach their ends.
There are 2 independent parts, one for each index of `grp`. The reference program is written for one: setup_inputs(seed, part) draws one part's arguments, and reference() takes and returns one part's arrays. A program takes and returns all parts, laid end to end along the dimension named above; an argument that names none is the same for every part. Nothing has to cross between parts.
All inputs are finite; a program needn't handle non-finite values.
Results may differ from the reference program's by a relative error of at most 0.0048.
Values may be sent and summed in bfloat16 or wider, within the bound.
A program may use at most 64 MiB of HBM per device.

```python
import math
import jax
import jax.numpy as jnp
from jax import lax

HEADS = 8
HEAD_DIM = 160
CHANNELS = 256
TILE_ROWS = 8
TILE_COLS = 16
INNER = 1280
WIN_TOKENS = 128
WIN_ROWS = 8
WIN_COLS = 8


def paired_draw(key):
    layout = (WIN_ROWS * WIN_COLS, WIN_TOKENS, HEADS, HEAD_DIM)
    key_draw = 1.41 * jax.random.truncated_normal(jax.random.fold_in(key, 11), -6.0, 6.0, layout, jnp.float32)
    query_draw = 1.41 * jax.random.truncated_normal(jax.random.fold_in(key, 12), -6.0, 6.0, layout, jnp.float32)
    final = (WIN_ROWS, WIN_COLS, WIN_TOKENS, HEADS * HEAD_DIM)
    return (query_draw.reshape(final).astype(jnp.bfloat16), key_draw.reshape(final).astype(jnp.bfloat16))


def draw_query_window(key, part):
    return paired_draw(jax.random.fold_in(key, 101))[0]


def draw_key_window(key, part):
    return paired_draw(jax.random.fold_in(key, 101))[1]


def draw_query_index(key, part):
    return paired_draw(jax.random.fold_in(key, 202))[0]


def draw_key_index(key, part):
    return paired_draw(jax.random.fold_in(key, 202))[1]


def steps_of(stream_key, dims, pieces, low, top_value):
    loudness = 1.0
    for position, parts in pieces:
        heights = jax.random.uniform(jax.random.fold_in(jax.random.fold_in(stream_key, 6), position), (parts,), jnp.float32, low / len(pieces), top_value / len(pieces))
        loudness = loudness * jnp.repeat(jnp.exp(heights), dims[position] // parts).reshape((-1,) + (1,) * (len(dims) - 1 - position))
    return loudness


def scatter_about(stream_key, extent, spread, reach, cuts=(), held_as=jnp.bfloat16):
    drawn = spread * jax.random.normal(stream_key, extent, jnp.float32)
    if cuts:
        drawn = drawn * steps_of(stream_key, extent, cuts, -0.22, 0.18)
    return jnp.clip(drawn, -reach, reach).astype(held_as)


def setup_inputs(seed: int = 0, part: int = 0) -> dict:
    keys = jax.random.split(jax.random.key(seed), 12)
    part_keys = jax.random.split(jax.random.fold_in(keys[11], part), 12)
    return {
        "query_window": draw_query_window(jax.random.fold_in(jax.random.fold_in(keys[11], part), 71), part),
        "key_window": draw_key_window(jax.random.fold_in(jax.random.fold_in(keys[11], part), 71), part),
        "value_window": scatter_about(part_keys[2], (WIN_ROWS, WIN_COLS, WIN_TOKENS, INNER), 1.0, 6.0, ((0, 8), (1, 2))),
        "query_index": draw_query_index(jax.random.fold_in(jax.random.fold_in(keys[11], part), 71), part),
        "key_index": draw_key_index(jax.random.fold_in(jax.random.fold_in(keys[11], part), 71), part),
        "proj_weight": scatter_about(keys[5], (INNER, 4 * CHANNELS), (INNER // 8) ** -0.5, 0.5),
        "proj_bias": scatter_about(keys[6], (4 * CHANNELS,), 0.5, 3.0, (), jnp.float32),
        "first_kernel": scatter_about(keys[7], (3, 3, CHANNELS, CHANNELS), (9 * CHANNELS) ** -0.5, 0.125),
        "first_bias": scatter_about(keys[8], (CHANNELS,), 0.5, 3.0, (), jnp.float32),
        "second_kernel": scatter_about(keys[9], (3, 3, CHANNELS, CHANNELS), (9 * CHANNELS) ** -0.5, 0.125),
        "second_bias": scatter_about(keys[10], (CHANNELS,), 0.5, 3.0, (), jnp.float32),
    }


def attend(queries, key_rows, values):
    scores = jnp.einsum('blhd,bmhd->bhlm', queries.astype(jnp.float32), key_rows.astype(jnp.float32)) / math.sqrt(HEAD_DIM)
    highest = lax.optimization_barrier(jnp.max(scores, axis=-1, keepdims=True))
    raised = jnp.exp(scores - highest)
    weights = (raised / lax.optimization_barrier(jnp.sum(raised, axis=-1, keepdims=True))).astype(jnp.bfloat16)
    mixed = jnp.einsum('bhlm,bmhd->blhd', weights.astype(jnp.float32), values.astype(jnp.float32))
    return mixed.astype(jnp.bfloat16)

def convolve(image, kernel, bias):
    height, breadth, depth = image.shape
    padded = jnp.pad(image, ((1, 1), (1, 1), (0, 0)))
    total = jnp.zeros((height * breadth, kernel.shape[-1]), jnp.float32)
    for row_shift in range(3):
        for col_shift in range(3):
            cells = padded[row_shift:row_shift + height, col_shift:col_shift + breadth].reshape(-1, depth)
            total = total + jnp.dot(cells, kernel[row_shift, col_shift], preferred_element_type=jnp.float32)
    return (total + bias).reshape(height, breadth, -1)

def reference(query_window, key_window, value_window, query_index, key_index, proj_weight, proj_bias, first_kernel, first_bias, second_kernel, second_bias):
    layout = (WIN_ROWS * WIN_COLS, WIN_TOKENS, HEADS, HEAD_DIM)
    window_out = attend(query_window.reshape(layout), key_window.reshape(layout), value_window.reshape(layout))
    index_out = attend(jnp.swapaxes(query_index.reshape(layout), 0, 1), jnp.swapaxes(key_index.reshape(layout), 0, 1), jnp.swapaxes(window_out, 0, 1))
    index_rows = jnp.swapaxes(index_out, 0, 1).reshape(-1, HEADS * HEAD_DIM)
    projected = (jnp.dot(index_rows, proj_weight, preferred_element_type=jnp.float32) + proj_bias).astype(jnp.bfloat16)
    grouped = projected.reshape(WIN_ROWS, WIN_COLS, TILE_ROWS, TILE_COLS, 2, 2, CHANNELS)
    shuffled = jnp.transpose(grouped, (0, 2, 4, 1, 3, 5, 6)).reshape(WIN_ROWS * TILE_ROWS * 2, WIN_COLS * TILE_COLS * 2, CHANNELS)
    activated = jax.nn.gelu(convolve(shuffled, first_kernel, first_bias)).astype(jnp.bfloat16)
    return convolve(activated, second_kernel, second_bias).astype(jnp.bfloat16)
```

```python
import functools
import math

import jax
import jax.numpy as jnp
from jax import lax
from jax.experimental import pallas as pl
from jax.experimental.pallas import tpu as pltpu
from jax.sharding import PartitionSpec as P

HEADS = 8
HEAD_DIM = 160
CHANNELS = 256
TILE_ROWS = 8
TILE_COLS = 16
LANES = 128


def extended(value, sides, width):
    for axis, dim in sides:
        size, length = (lax.axis_size(axis), value.shape[dim])
        up = [(i, (i + 1) % size) for i in range(size - 1)]
        down = [(j, i) for i, j in up]
        last = lax.slice_in_dim(value, length - width, length, axis=dim)
        first = lax.slice_in_dim(value, 0, width, axis=dim)
        before = lax.ppermute(last, axis, up)
        after = lax.ppermute(first, axis, down)
        value = jnp.concatenate([before, value, after], axis=dim)
    return value


def softmax_rows(scores):
    highest = jnp.max(scores, axis=-1, keepdims=True)
    raised = jnp.exp(scores - highest)
    return (raised / jnp.sum(raised, axis=-1, keepdims=True)).astype(jnp.bfloat16)


def window_attend(queries, key_rows, values):
    scores = jnp.einsum(
        "blhd,bmhd->bhlm", queries, key_rows, preferred_element_type=jnp.float32
    ) / math.sqrt(HEAD_DIM)
    weights = softmax_rows(scores)
    return jnp.einsum(
        "bhlm,bmhd->blhd", weights, values, preferred_element_type=jnp.float32
    ).astype(jnp.bfloat16)


def index_attend(queries, key_rows, values):
    scores = jnp.einsum(
        "lbhd,mbhd->bhlm", queries, key_rows, preferred_element_type=jnp.float32
    ) / math.sqrt(HEAD_DIM)
    weights = softmax_rows(scores)
    return jnp.einsum(
        "bhlm,mbhd->lbhd", weights, values, preferred_element_type=jnp.float32
    ).astype(jnp.bfloat16)


def convolve(image, kernel, bias):
    height, breadth, depth = image.shape
    padded = extended(image, (("row", 0), ("col", 1)), 1)
    total = jnp.zeros((height * breadth, kernel.shape[-1]), jnp.float32)
    for row_shift in range(3):
        for col_shift in range(3):
            cells = padded[row_shift : row_shift + height, col_shift : col_shift + breadth].reshape(
                -1, depth
            )
            total = total + jnp.dot(
                cells, kernel[row_shift, col_shift], preferred_element_type=jnp.float32
            )
    return (total + bias).reshape(height, breadth, -1)


def attend_heads(queries, key_part, value_part, same):
    rows, features = queries.shape
    head_dim = features // HEADS
    factor = math.log2(math.e) / math.sqrt(head_dim)
    blocks = [None] * (features // LANES)
    for head in range(HEADS):
        low, high = (head * head_dim, (head + 1) * head_dim)
        start, stop = (low // LANES * LANES, -(-high // LANES) * LANES)
        lane = lax.broadcasted_iota(jnp.int32, (rows, stop - start), 1) + start
        inside = (lane >= low) & (lane < high)
        part = queries[:, start:stop]
        part = jnp.where(inside, part, jnp.zeros_like(part))
        scores = lax.dot_general(
            part,
            key_part(start, stop),
            (((1,), (1,)), ((), ())),
            preferred_element_type=jnp.float32,
        )
        if same is not None:
            scores = jnp.where(same, scores, -1e30)
        highest = jnp.max(scores, axis=-1, keepdims=True)
        raised = jnp.exp2((scores - highest) * factor)
        weights = (raised * (1.0 / jnp.sum(raised, axis=-1, keepdims=True))).astype(jnp.bfloat16)
        mixed = jnp.dot(weights, value_part(start, stop), preferred_element_type=jnp.float32)
        mixed = jnp.where(inside, mixed, 0.0)
        for block in range(start // LANES, stop // LANES):
            piece = mixed[:, block * LANES - start : (block + 1) * LANES - start]
            blocks[block] = piece if blocks[block] is None else blocks[block] + piece
    return jnp.concatenate(blocks, axis=1).astype(jnp.bfloat16)


def attention_kernel(
    count_row,
    count_col,
    qw_hbm,
    kw_hbm,
    vw_hbm,
    qi_hbm,
    ki_hbm,
    pw_hbm,
    fk_hbm,
    sk_hbm,
    pb_ref,
    fb_ref,
    sb_ref,
    out_ref,
    qw,
    kw,
    vw,
    pw,
    window_out,
    k_all,
    v_all,
    q_all,
    proj,
    field,
    fk,
    sk,
    halo_up,
    halo_down,
    side_right,
    side_left,
    shuffled,
    activated,
    load_sem,
    own_sem,
    q_own_sem,
    out_own_sem,
    k_send,
    k_recv,
    v_send,
    v_recv,
    q_send,
    q_recv,
    r_send,
    r_recv,
    edge_send,
    edge_recv,
    side_send,
    side_recv,
):
    count = count_row * count_col
    windows = qw.shape[0]
    owned = k_all.shape[2]
    features = qw.shape[2]
    me = lax.axis_index("row") * count_col + lax.axis_index("col")

    def offset(step):
        half = (step + 1) // 2
        return count // 2 + jnp.where(step % 2 == 1, half, -half)

    def peer_of(shift):
        return lax.rem(me + shift, count)

    def device(peer):
        return {"row": peer // count_col, "col": lax.rem(peer, count_col)}

    def tokens(peer):
        return pl.ds(pl.multiple_of(peer * owned, owned), owned)

    def copy_k(shift):
        peer = peer_of(shift)
        return pltpu.make_async_remote_copy(
            src_ref=ki_hbm.at[:, tokens(peer), :],
            dst_ref=k_all.at[me],
            send_sem=k_send.at[shift],
            recv_sem=k_recv.at[shift],
            device_id=device(peer),
            device_id_type=pl.DeviceIdType.MESH,
        )

    def copy_v(shift):
        peer = peer_of(shift)
        return pltpu.make_async_remote_copy(
            src_ref=window_out.at[:, tokens(peer), :],
            dst_ref=v_all.at[me],
            send_sem=v_send.at[shift],
            recv_sem=v_recv.at[shift],
            device_id=device(peer),
            device_id_type=pl.DeviceIdType.MESH,
        )

    def copy_q(window, shift):
        peer = peer_of(shift)
        return pltpu.make_async_remote_copy(
            src_ref=qi_hbm.at[window, tokens(peer), :],
            dst_ref=q_all.at[window, me],
            send_sem=q_send.at[window, shift],
            recv_sem=q_recv.at[window, shift],
            device_id=device(peer),
            device_id_type=pl.DeviceIdType.MESH,
        )

    def copy_r(window, shift):
        peer = peer_of(shift)
        return pltpu.make_async_remote_copy(
            src_ref=proj.at[window, tokens(peer), :],
            dst_ref=field.at[window, tokens(me), :],
            send_sem=r_send.at[window, shift],
            recv_sem=r_recv.at[window, shift],
            device_id=device(peer),
            device_id_type=pl.DeviceIdType.MESH,
        )

    def own_q(window):
        return pltpu.make_async_copy(
            qi_hbm.at[window, tokens(me), :], q_all.at[window, me], q_own_sem.at[window]
        )

    def own_r(window):
        return pltpu.make_async_copy(
            proj.at[window, tokens(me), :],
            field.at[window, tokens(me), :],
            out_own_sem.at[window],
        )

    def each_shift(body):
        def step(index, carry):
            body(offset(index))
            return carry

        lax.fori_loop(0, count - 1, step, 0)

    barrier = pltpu.get_barrier_semaphore()

    def greet(shift):
        pl.semaphore_signal(
            barrier,
            inc=1,
            device_id=device(peer_of(shift)),
            device_id_type=pl.DeviceIdType.MESH,
        )

    each_shift(greet)

    loads = [
        pltpu.make_async_copy(source, target, load_sem.at[place])
        for place, (source, target) in enumerate(
            (
                (qw_hbm, qw),
                (kw_hbm, kw),
                (vw_hbm, vw),
                (pw_hbm, pw),
                (fk_hbm, fk),
                (sk_hbm, sk),
            )
        )
    ]
    for load in loads:
        load.start()
    own_k = pltpu.make_async_copy(ki_hbm.at[:, tokens(me), :], k_all.at[me], own_sem.at[0])
    own_k.start()

    def each_window(body):
        def step(index, carry):
            body(index)
            return carry

        lax.fori_loop(0, windows, step, 0)

    each_window(lambda window: own_q(window).start())
    for halo in (halo_up, halo_down, side_right, side_left):
        halo[...] = jnp.zeros_like(halo)
    pl.semaphore_wait(barrier, count - 1)
    each_shift(lambda shift: copy_k(shift).start())


    for load in loads:
        load.wait()

    def within(window):
        window_out[window] = attend_heads(
            qw[window],
            lambda start, stop: kw[window, :, start:stop],
            lambda start, stop: vw[window, :, start:stop],
            None,
        )

    each_window(within)
    own_v = pltpu.make_async_copy(
        window_out.at[:, tokens(me), :], v_all.at[me], own_sem.at[1]
    )
    own_v.start()
    each_shift(lambda shift: copy_v(shift).start())
    each_window(lambda window: each_shift(lambda shift: copy_q(window, shift).start()))

    own_k.wait()
    own_v.wait()
    each_shift(lambda shift: copy_k(shift).wait())
    each_shift(lambda shift: copy_v(shift).wait())

    key_rows = k_all.reshape(count * windows * owned, features)
    value_rows = v_all.reshape(count * windows * owned, features)
    query_rows = q_all.reshape(windows, count * owned, features)
    square = (count * owned, count * windows * owned)
    same = lax.rem(lax.broadcasted_iota(jnp.int32, square, 0), owned) == lax.rem(
        lax.broadcasted_iota(jnp.int32, square, 1), owned
    )

    def across(window):
        own_q(window).wait()
        each_shift(lambda shift: copy_q(window, shift).wait())
        mixed = attend_heads(
            query_rows[window],
            lambda start, stop: key_rows[:, start:stop],
            lambda start, stop: value_rows[:, start:stop],
            same,
        )
        rows = jnp.dot(mixed, pw[...], preferred_element_type=jnp.float32) + pb_ref[...]
        proj[window] = rows.astype(jnp.bfloat16)
        own_r(window).start()
        each_shift(lambda shift: copy_r(window, shift).start())

    each_window(across)

    my_row, my_col = (lax.axis_index("row"), lax.axis_index("col"))
    has_up, has_down = (my_row > 0, my_row < count_row - 1)
    has_left, has_right = (my_col > 0, my_col < count_col - 1)
    tokens_win = field.shape[1]
    tile = TILE_COLS

    def copy_to(source, target, sems, step_row, step_col):
        return pltpu.make_async_remote_copy(
            src_ref=source,
            dst_ref=target,
            send_sem=sems[0],
            recv_sem=sems[1],
            device_id={"row": my_row + step_row, "col": my_col + step_col},
            device_id_type=pl.DeviceIdType.MESH,
        )

    def edge(window, down):
        source = pl.ds(tokens_win - tile if down else 0, tile)
        target = halo_up if down else halo_down
        place = 0 if down else 1
        return copy_to(
            field.at[window, source, :],
            target.at[window],
            (edge_send.at[place, window], edge_recv.at[place, window]),
            1 if down else -1,
            0,
        )

    def side(right, step_row):
        window = windows - 1 if right else 0
        target = side_left if right else side_right
        place = (0 if right else 3) + step_row + 1
        if step_row == 0:
            source, rows = (pl.ds(0, tokens_win), pl.ds(tile, tokens_win))
        elif step_row > 0:
            source, rows = (pl.ds(tokens_win - tile, tile), pl.ds(0, tile))
        else:
            source, rows = (pl.ds(0, tile), pl.ds(tokens_win + tile, tile))
        return copy_to(
            field.at[window, source, :],
            target.at[rows, :],
            (side_send.at[place], side_recv.at[place]),
            step_row,
            1 if right else -1,
        )

    row_ways = ((0, None, None), (1, has_down, has_up), (-1, has_up, has_down))

    def send_sides(right):
        there = has_right if right else has_left
        for step_row, goes, _ in row_ways:

            @pl.when(there if goes is None else there & goes)
            def _():
                side(right, step_row).start()

    def finish(window):
        own_r(window).wait()
        each_shift(lambda shift: copy_r(window, shift).wait())
        for down, goes in ((True, has_down), (False, has_up)):

            @pl.when(goes)
            def _():
                edge(window, down).start()

    finish(0)
    send_sides(False)

    def later(window, carry):
        finish(window)
        return carry

    lax.fori_loop(1, windows, later, 0)
    send_sides(True)

    depth = fk.shape[-1]
    width = (windows + 1) * tile
    token_rows = tokens_win // tile
    total = shuffled.shape[1]

    for window in range(windows):
        for line in range(token_rows):
            start = tile + (line + 1) * width + window * tile
            for parity in range(2):
                shuffled[parity, start : start + tile, depth : 3 * depth] = field[
                    window,
                    line * tile : (line + 1) * tile,
                    parity * 2 * depth : (parity + 1) * 2 * depth,
                ]

    for window in range(windows):
        for down, goes, comes in ((True, has_down, has_up), (False, has_up, has_down)):

            @pl.when(goes)
            def _():
                edge(window, down).wait_send()

            @pl.when(comes)
            def _():
                edge(window, down).wait_recv()

    for right in (True, False):
        there, here = (has_right, has_left) if right else (has_left, has_right)
        for step_row, goes, comes in row_ways:

            @pl.when(there if goes is None else there & goes)
            def _():
                side(right, step_row).wait_send()

            @pl.when(here if comes is None else here & comes)
            def _():
                side(right, step_row).wait_recv()

    for parity in range(2):
        lanes = slice(parity * 2 * depth, (parity + 1) * 2 * depth)
        for window in range(windows):
            for source, line in ((halo_up, 0), (halo_down, token_rows + 1)):
                start = tile + line * width + window * tile
                shuffled[parity, start : start + tile, depth : 3 * depth] = source[
                    window, :, lanes
                ]
        first = lax.broadcasted_iota(jnp.int32, (tile, 2 * depth), 0) < tile // 2
        shuffled[parity, 0:tile, depth : 3 * depth] = side_left[0:tile, lanes]
        for line in range(token_rows + 2):
            start = tile + line * width + windows * tile
            block = side_right[line * tile : (line + 1) * tile, lanes]
            if line < token_rows + 1:
                after = side_left[(line + 1) * tile : (line + 2) * tile, lanes]
                block = jnp.where(first, block, after)
            shuffled[parity, start : start + tile, depth : 3 * depth] = block
        odd = shuffled[parity, :, 2 * depth : 3 * depth].astype(jnp.float32)
        shuffled[parity, :, 0:depth] = pltpu.roll(odd, 1, 0).astype(jnp.bfloat16)
        even = shuffled[parity, :, depth : 2 * depth].astype(jnp.float32)
        shuffled[parity, :, 3 * depth :] = pltpu.roll(even, total - 1, 0).astype(jnp.bfloat16)

    def convolve_rows(source, weights, row_parity, col_parity, start, size):
        if row_parity == 0:
            taps = ((1, -width), (0, 0), (1, 0))
        else:
            taps = ((0, 0), (1, 0), (0, width))
        result = None
        for tap, (parity, shift) in enumerate(taps):
            cells = source[
                parity,
                start + shift : start + shift + size,
                col_parity * depth : (col_parity + 3) * depth,
            ]
            part = jnp.dot(cells, weights[tap], preferred_element_type=jnp.float32)
            result = part if result is None else result + part
        return result

    size = total - width
    main = windows * tile
    right_stop = jnp.where(has_right, main + tile // 2, main)
    left_start = jnp.where(has_left, main + tile // 2, width)
    line_start = jnp.where(has_up, 0, 1)
    line_stop = jnp.where(has_down, token_rows + 2, token_rows + 1)
    for parity in range(2):
        start = width if parity == 0 else 0
        place = lax.broadcasted_iota(jnp.int32, (size, depth), 0) + start
        column = lax.rem(place + (width - tile), width)
        line = lax.div(place + (width - tile) + tile // 2, width) - 1
        valid = (column < right_stop) | (column >= left_start)
        valid = valid & ((line < line_stop) if parity == 0 else (line >= line_start))
        for other in range(2):
            value = convolve_rows(shuffled, fk, parity, other, start, size) + fb_ref[...]
            value = jnp.where(valid, jax.nn.gelu(value), 0.0)
            rows = slice(start, start + size)
            activated[parity, rows, (other + 1) * depth : (other + 2) * depth] = value.astype(
                jnp.bfloat16
            )
            if other == 1:
                moved = pltpu.roll(value, 1, 0)
                activated[parity, rows, 0:depth] = moved.astype(jnp.bfloat16)
            else:
                moved = pltpu.roll(value, size - 1, 0)
                activated[parity, rows, 3 * depth :] = moved.astype(jnp.bfloat16)

    for parity in range(2):
        for other in range(2):
            value = convolve_rows(
                activated, sk, parity, other, tile + width, token_rows * width
            )
            value = (value + sb_ref[...]).astype(jnp.bfloat16)
            for line in range(token_rows):
                out_ref[2 * line + parity, :, other * depth : (other + 1) * depth] = value[
                    line * width : line * width + windows * tile
                ]


def fused(qw, kw, vw, qi, ki, proj_weight, proj_bias, first_kernel, first_bias, second_kernel, second_bias):
    windows, tokens_win, features = qw.shape
    count_row = lax.axis_size("row")
    count_col = lax.axis_size("col")
    count = count_row * count_col
    owned = tokens_win // count
    channels = proj_weight.shape[-1]
    depth = first_kernel.shape[-1]
    taps = (first_kernel.shape[0], first_kernel.shape[1] * first_kernel.shape[2], depth)
    token_rows = tokens_win // TILE_COLS
    width = (windows + 1) * TILE_COLS
    planes = (2, TILE_COLS + (token_rows + 2) * width, 4 * depth)
    whole = pl.BlockSpec(memory_space=pl.ANY)
    held = pl.BlockSpec(memory_space=pltpu.VMEM)
    dma = pltpu.SemaphoreType.DMA
    return pl.pallas_call(
        functools.partial(attention_kernel, count_row, count_col),
        out_shape=jax.ShapeDtypeStruct(
            (2 * token_rows, windows * TILE_COLS, 2 * depth), jnp.bfloat16
        ),
        in_specs=[whole] * 8 + [held] * 3,
        out_specs=held,
        scratch_shapes=[
            pltpu.VMEM(qw.shape, jnp.bfloat16),
            pltpu.VMEM(qw.shape, jnp.bfloat16),
            pltpu.VMEM(qw.shape, jnp.bfloat16),
            pltpu.VMEM(proj_weight.shape, jnp.bfloat16),
            pltpu.VMEM(qw.shape, jnp.bfloat16),
            pltpu.VMEM((count, windows, owned, features), jnp.bfloat16),
            pltpu.VMEM((count, windows, owned, features), jnp.bfloat16),
            pltpu.VMEM((windows, count, owned, features), jnp.bfloat16),
            pltpu.VMEM((windows, tokens_win, channels), jnp.bfloat16),
            pltpu.VMEM((windows, tokens_win, channels), jnp.bfloat16),
            pltpu.VMEM(taps, jnp.bfloat16),
            pltpu.VMEM(taps, jnp.bfloat16),
            pltpu.VMEM((windows, TILE_COLS, channels), jnp.bfloat16),
            pltpu.VMEM((windows, TILE_COLS, channels), jnp.bfloat16),
            pltpu.VMEM((tokens_win + 2 * TILE_COLS, channels), jnp.bfloat16),
            pltpu.VMEM((tokens_win + 2 * TILE_COLS, channels), jnp.bfloat16),
            pltpu.VMEM(planes, jnp.bfloat16),
            pltpu.VMEM(planes, jnp.bfloat16),
            dma((6,)),
            dma((2,)),
            dma((windows,)),
            dma((windows,)),
            dma((count,)),
            dma((count,)),
            dma((count,)),
            dma((count,)),
            dma((windows, count)),
            dma((windows, count)),
            dma((windows, count)),
            dma((windows, count)),
            dma((2, windows)),
            dma((2, windows)),
            dma((6,)),
            dma((6,)),
        ],
        compiler_params=pltpu.CompilerParams(
            collective_id=0, has_side_effects=True, vmem_limit_bytes=62 * 1024 * 1024
        ),
    )(
        qw,
        kw,
        vw,
        qi,
        ki,
        proj_weight,
        first_kernel.reshape(taps),
        second_kernel.reshape(taps),
        proj_bias.reshape(1, channels),
        first_bias.reshape(1, depth),
        second_bias.reshape(1, depth),
    )


def convolutions(
    projected, rows_dev, cols_dev, first_kernel, first_bias, second_kernel, second_bias
):
    grouped = projected.reshape(rows_dev, cols_dev, TILE_ROWS, TILE_COLS, 2, 2, CHANNELS)
    shuffled = jnp.transpose(grouped, (0, 2, 4, 1, 3, 5, 6)).reshape(
        rows_dev * TILE_ROWS * 2, cols_dev * TILE_COLS * 2, CHANNELS
    )
    activated = jax.nn.gelu(convolve(shuffled, first_kernel, first_bias)).astype(jnp.bfloat16)
    return convolve(activated, second_kernel, second_bias).astype(jnp.bfloat16)


def shards(
    query_window,
    key_window,
    value_window,
    query_index,
    key_index,
    proj_weight,
    proj_bias,
    first_kernel,
    first_bias,
    second_kernel,
    second_bias,
):
    rows_dev, cols_dev, tokens_win, features = query_window.shape
    flat = (rows_dev * cols_dev, tokens_win, features)
    owners = lax.axis_size("row") * lax.axis_size("col")
    if rows_dev == 1 and tokens_win % (owners * 8) == 0 and features % LANES == 0:
        fine = fused(
            query_window.reshape(flat),
            key_window.reshape(flat),
            value_window.reshape(flat),
            query_index.reshape(flat),
            key_index.reshape(flat),
            proj_weight,
            proj_bias,
            first_kernel,
            first_bias,
            second_kernel,
            second_bias,
        )
        return fine.reshape(fine.shape[0], 2 * fine.shape[1], -1)
    layout = (rows_dev * cols_dev, tokens_win, HEADS, HEAD_DIM)
    window_out = window_attend(
        query_window.reshape(layout), key_window.reshape(layout), value_window.reshape(layout)
    ).reshape(query_window.shape)
    count_row = lax.axis_size("row")
    count_col = lax.axis_size("col")
    owned_tokens = tokens_win // (count_row * count_col)
    moved = (
        lax.all_to_all(query_index, ("row", "col"), split_axis=2, concat_axis=0, tiled=True),
        lax.all_to_all(key_index, ("row", "col"), split_axis=2, concat_axis=0, tiled=True),
        lax.all_to_all(window_out, ("row", "col"), split_axis=2, concat_axis=0, tiled=True),
    )
    owner_shape = moved[0].shape
    across = (-1, owned_tokens, HEADS, HEAD_DIM)
    index_out = index_attend(
        moved[0].reshape(across), moved[1].reshape(across), moved[2].reshape(across)
    )
    index_rows = index_out.reshape(-1, features)
    owner_rows = (
        jnp.dot(index_rows, proj_weight, preferred_element_type=jnp.float32) + proj_bias
    ).astype(jnp.bfloat16)
    last = owner_rows.shape[-1]
    shaped = owner_rows.reshape(tuple(owner_shape[:-1]) + (last,))
    returned = lax.all_to_all(shaped, ("row", "col"), split_axis=0, concat_axis=2, tiled=True)
    projected = returned.reshape(rows_dev * cols_dev * tokens_win, last)
    return convolutions(
        projected, rows_dev, cols_dev, first_kernel, first_bias, second_kernel, second_bias
    )


def solution(mesh):
    in_specs = (
        P(("grp", "row"), "col", None, None),
        P(("grp", "row"), "col", None, None),
        P(("grp", "row"), "col", None, None),
        P(("grp", "row"), "col", None, None),
        P(("grp", "row"), "col", None, None),
        P(),
        P(),
        P(),
        P(),
        P(),
        P(),
    )
    out_specs = P(("grp", "row"), "col", None)
    return jax.shard_map(shards, mesh=mesh, in_specs=in_specs, out_specs=out_specs, check_vma=False)
```

```python
import functools
import math

import jax
import jax.numpy as jnp
from jax import lax
from jax.experimental import pallas as pl
from jax.experimental.pallas import tpu as pltpu
from jax.sharding import PartitionSpec as P

HEADS = 8
HEAD_DIM = 160
CHANNELS = 256
TILE_ROWS = 8
TILE_COLS = 16
LANES = 128
LINES = 2
PIECES = 4


def extended(value, sides, width):
    for axis, dim in sides:
        size, length = (lax.axis_size(axis), value.shape[dim])
        up = [(i, (i + 1) % size) for i in range(size - 1)]
        down = [(j, i) for i, j in up]
        last = lax.slice_in_dim(value, length - width, length, axis=dim)
        first = lax.slice_in_dim(value, 0, width, axis=dim)
        before = lax.ppermute(last, axis, up)
        after = lax.ppermute(first, axis, down)
        value = jnp.concatenate([before, value, after], axis=dim)
    return value


def softmax_rows(scores):
    highest = jnp.max(scores, axis=-1, keepdims=True)
    raised = jnp.exp(scores - highest)
    return (raised / jnp.sum(raised, axis=-1, keepdims=True)).astype(jnp.bfloat16)


def window_attend(queries, key_rows, values):
    scores = jnp.einsum(
        "blhd,bmhd->bhlm", queries, key_rows, preferred_element_type=jnp.float32
    ) / math.sqrt(HEAD_DIM)
    weights = softmax_rows(scores)
    return jnp.einsum(
        "bhlm,bmhd->blhd", weights, values, preferred_element_type=jnp.float32
    ).astype(jnp.bfloat16)


def index_attend(queries, key_rows, values):
    scores = jnp.einsum(
        "lbhd,mbhd->bhlm", queries, key_rows, preferred_element_type=jnp.float32
    ) / math.sqrt(HEAD_DIM)
    weights = softmax_rows(scores)
    return jnp.einsum(
        "bhlm,mbhd->lbhd", weights, values, preferred_element_type=jnp.float32
    ).astype(jnp.bfloat16)


def convolve(image, kernel, bias):
    height, breadth, depth = image.shape
    padded = extended(image, (("row", 0), ("col", 1)), 1)
    total = jnp.zeros((height * breadth, kernel.shape[-1]), jnp.float32)
    for row_shift in range(3):
        for col_shift in range(3):
            cells = padded[row_shift : row_shift + height, col_shift : col_shift + breadth].reshape(
                -1, depth
            )
            total = total + jnp.dot(
                cells, kernel[row_shift, col_shift], preferred_element_type=jnp.float32
            )
    return (total + bias).reshape(height, breadth, -1)


def attend_heads(queries, key_part, value_part, same):
    rows, features = queries.shape
    head_dim = features // HEADS
    factor = math.log2(math.e) / math.sqrt(head_dim)
    blocks = [None] * (features // LANES)
    for head in range(HEADS):
        low, high = (head * head_dim, (head + 1) * head_dim)
        start, stop = (low // LANES * LANES, -(-high // LANES) * LANES)
        lane = lax.broadcasted_iota(jnp.int32, (rows, stop - start), 1) + start
        inside = (lane >= low) & (lane < high)
        part = queries[:, start:stop]
        part = jnp.where(inside, part, jnp.zeros_like(part))
        scores = lax.dot_general(
            part,
            key_part(start, stop),
            (((1,), (1,)), ((), ())),
            preferred_element_type=jnp.float32,
        )
        if same is not None:
            scores = jnp.where(same, scores, -1e30)
        highest = jnp.max(scores, axis=-1, keepdims=True)
        raised = jnp.exp2((scores - highest) * factor)
        weights = (raised * (1.0 / jnp.sum(raised, axis=-1, keepdims=True))).astype(jnp.bfloat16)
        mixed = jnp.dot(weights, value_part(start, stop), preferred_element_type=jnp.float32)
        mixed = jnp.where(inside, mixed, 0.0)
        for block in range(start // LANES, stop // LANES):
            piece = mixed[:, block * LANES - start : (block + 1) * LANES - start]
            blocks[block] = piece if blocks[block] is None else blocks[block] + piece
    return jnp.concatenate(blocks, axis=1).astype(jnp.bfloat16)


def one_hot(target, shape):
    return (lax.broadcasted_iota(jnp.int32, shape, 1) == target).astype(jnp.bfloat16)


def pick(rows, source):
    return jnp.dot(rows, source, preferred_element_type=jnp.float32).astype(jnp.bfloat16)


def attention_kernel(
    count_row,
    count_col,
    qw_hbm,
    kw_hbm,
    vw_hbm,
    qi_hbm,
    ki_hbm,
    pw_hbm,
    fk_hbm,
    sk_hbm,
    pb_ref,
    fb_ref,
    sb_ref,
    out_hbm,
    qw,
    kw,
    vw,
    qi,
    ki,
    pw,
    fk,
    sk,
    window_out,
    k_mine,
    q_mine,
    v_mine,
    k_all,
    q_all,
    v_all,
    proj,
    field,
    seam_mine,
    seam_all,
    places,
    slides,
    shuffled,
    activated,
    stage,
    out,
    load_sem,
    k_send,
    k_recv,
    q_send,
    q_recv,
    v_send,
    v_recv,
    r_send,
    r_recv,
    side_send,
    side_recv,
    edge_send,
    edge_recv,
    seam_send,
    seam_recv,
    share_sem,
    out_sem,
):
    count = count_row * count_col
    half = count // 2
    windows, tokens_win, features = qw.shape
    tile = TILE_COLS
    token_rows = tokens_win // tile
    chunks, _, block, channels = proj.shape
    pair = block // windows
    wide = windows * tile
    width = shuffled.shape[2]
    depth = fk.shape[-1]
    my_row, my_col = (lax.axis_index("row"), lax.axis_index("col"))
    me = my_row * count_col + my_col
    my_half, my_place = (me // half, lax.rem(me, half))

    def peer_of(step):
        across = (1 - my_half) * half + lax.rem(my_place + step, half)
        beside = my_half * half + lax.rem(my_place + step + 1, half)
        return jnp.where(step < half, across, beside)

    def device(peer):
        return {"row": peer // count_col, "col": lax.rem(peer, count_col)}

    def each_peer(body):
        def step(index, carry):
            body(index)
            return carry

        lax.fori_loop(0, count - 1, step, 0)

    barrier = pltpu.get_barrier_semaphore()

    def greet(step):
        pl.semaphore_signal(
            barrier,
            inc=1,
            device_id=device(peer_of(step)),
            device_id_type=pl.DeviceIdType.MESH,
        )

    each_peer(greet)

    loads = [
        pltpu.make_async_copy(source, target, load_sem.at[place])
        for place, (source, target) in enumerate(
            (
                (ki_hbm, ki),
                (qi_hbm, qi),
                (qw_hbm, qw),
                (kw_hbm, kw),
                (vw_hbm, vw),
                (pw_hbm, pw),
                (fk_hbm, fk),
                (sk_hbm, sk),
            )
        )
    ]
    for load in loads:
        load.start()

    def sender(source, target, sems):
        def copy(chunk, step):
            peer = peer_of(step)
            return pltpu.make_async_remote_copy(
                src_ref=source.at[chunk, peer],
                dst_ref=target.at[chunk, me],
                send_sem=sems[0].at[chunk, step],
                recv_sem=sems[1].at[chunk, step],
                device_id=device(peer),
                device_id_type=pl.DeviceIdType.MESH,
            )

        return copy

    copy_k = sender(k_mine, k_all, (k_send, k_recv))
    copy_q = sender(q_mine, q_all, (q_send, q_recv))
    copy_v = sender(v_mine, v_all, (v_send, v_recv))
    copy_r = sender(proj, field, (r_send, r_recv))

    def flat(ref):
        return ref.reshape(chunks, count * block, ref.shape[-1])

    def order(chunk):
        shape = (count * block, windows * tokens_win)
        row = lax.broadcasted_iota(jnp.int32, shape, 0)
        place = lax.rem(row, pair)
        line = jnp.where(place == 0, chunk, token_rows - 1 - chunk)
        window = lax.div(lax.rem(row, block), pair)
        return one_hot(window * tokens_win + line * tile + lax.div(row, block), shape)

    ki_rows = ki.reshape(windows * tokens_win, features)
    qi_rows = qi.reshape(windows * tokens_win, features)
    out_rows = window_out.reshape(windows * tokens_win, features)

    def arrange(source, mine, everyone, chunk):
        flat(mine)[chunk] = pick(order(chunk), source[...])
        everyone[chunk, me] = mine[chunk, me]

    def send(copy, chunk, before=None):
        def step(index):
            if before is not None:
                for earlier, place in before:
                    earlier(place, index).wait_send()
            copy(chunk, index).start()

        each_peer(step)

    for line in (0, token_rows + 1):
        for parity in range(2):
            shuffled[parity, line] = jnp.zeros(shuffled.shape[2:], jnp.bfloat16)
    loads[0].wait()
    arrange(ki_rows, k_mine, k_all, 0)
    pl.semaphore_wait(barrier, count - 1)
    send(copy_k, 0)
    loads[1].wait()
    arrange(qi_rows, q_mine, q_all, 0)
    send(copy_q, 0)

    def next_pairs(chunk, carry):
        arrange(ki_rows, k_mine, k_all, chunk)
        arrange(qi_rows, q_mine, q_all, chunk)
        return carry

    lax.fori_loop(1, chunks, next_pairs, 0)

    for load in loads[2:]:
        load.wait()

    def within(window, carry):
        window_out[window] = attend_heads(
            qw[window],
            lambda start, stop: kw[window, :, start:stop],
            lambda start, stop: vw[window, :, start:stop],
            None,
        )
        return carry

    lax.fori_loop(0, windows, within, 0)

    def next_values(chunk, carry):
        arrange(out_rows, v_mine, v_all, chunk)
        return carry

    lax.fori_loop(0, chunks, next_values, 0)
    send(copy_v, 0)

    def send_chunk(chunk):
        for copy in (copy_k, copy_q, copy_v):
            send(copy, chunk, [(copy, chunk - 1)])

    send_chunk(1)

    square = (count * block, count * block)
    same = lax.rem(lax.broadcasted_iota(jnp.int32, square, 0), pair) == lax.rem(
        lax.broadcasted_iota(jnp.int32, square, 1), pair
    )

    def across(chunk):
        for copy in (copy_k, copy_q, copy_v):
            each_peer(lambda step: copy(chunk, step).wait_recv())
        mixed = attend_heads(
            flat(q_all)[chunk],
            lambda start, stop: flat(k_all)[chunk, :, start:stop],
            lambda start, stop: flat(v_all)[chunk, :, start:stop],
            same,
        )
        rows = jnp.dot(mixed, pw[...], preferred_element_type=jnp.float32) + pb_ref[...]
        flat(proj)[chunk] = rows.astype(jnp.bfloat16)
        field[chunk, me] = proj[chunk, me]

    has_up, has_down = (my_row > 0, my_row < count_row - 1)
    first_col = my_col == 0

    shape = (pair * width, (count + 1) * block)
    row = lax.broadcasted_iota(jnp.int32, shape, 0)
    slot, place = (lax.rem(row, width), lax.div(row, width))
    token = jnp.where(slot <= wide, slot, slot - width)

    def source_row(column):
        inside = (column >= 0) & (column < wide)
        own = lax.rem(column + tile, tile) * block + lax.div(column + tile, tile) * pair - pair
        right = jnp.where((column == wide) & first_col, count * block, -token_rows)
        left = jnp.where(
            (column == -1) & (my_col > 0), count * block + (windows - 1) * pair, right
        )
        return jnp.where(inside, own, left) + place

    for shift in range(3):
        places[shift] = one_hot(source_row(token + shift - 1), shape)
    shape = (width, width)
    row = lax.broadcasted_iota(jnp.int32, shape, 0)
    for way in range(2):
        slides[way] = one_hot(lax.rem(row + width + 2 * way - 1, width), shape)

    def line_of(chunk, place):
        return chunk + 1 if place == 0 else token_rows - chunk

    near = jnp.where(first_col, count - 1, 0)
    turn = lax.rem(my_place - lax.rem(near, half) + half, half)
    first_step = jnp.where(
        near // half == my_half, half + lax.rem(turn - 1 + half, half), turn
    )

    def side(chunk):
        return pltpu.make_async_remote_copy(
            src_ref=field.at[chunk, near],
            dst_ref=field.at[chunk, count],
            send_sem=side_send.at[chunk],
            recv_sem=side_recv.at[chunk],
            device_id={"row": my_row, "col": 1 - my_col},
            device_id_type=pl.DeviceIdType.MESH,
        )

    def edge(parity, down):
        lanes = pl.ds(depth, 2 * depth)
        source, target = (token_rows, 0) if down else (1, token_rows + 1)
        place = 2 * parity + (1 if down else 0)
        return pltpu.make_async_remote_copy(
            src_ref=shuffled.at[parity, source, :, lanes],
            dst_ref=shuffled.at[parity, target, :, lanes],
            send_sem=edge_send.at[place],
            recv_sem=edge_recv.at[place],
            device_id={"row": my_row + (1 if down else -1), "col": my_col},
            device_id_type=pl.DeviceIdType.MESH,
        )

    seam = count_row // 2
    above, below = (my_row == seam - 1, my_row == seam)

    def relay(way):
        return pltpu.make_async_remote_copy(
            src_ref=seam_mine.at[way],
            dst_ref=seam_all.at[my_row, my_col],
            send_sem=seam_send.at[way],
            recv_sem=seam_recv.at[my_row],
            device_id={"row": jnp.where(way == 0, seam, seam - 1), "col": my_col},
            device_id_type=pl.DeviceIdType.MESH,
        )

    def seam_wait(owner):
        pltpu.make_async_remote_copy(
            src_ref=seam_mine.at[0],
            dst_ref=seam_all.at[owner, my_col],
            send_sem=seam_send.at[0],
            recv_sem=seam_recv.at[owner],
            device_id={"row": my_row, "col": 1 - my_col},
            device_id_type=pl.DeviceIdType.MESH,
        ).wait_recv()

    def seam_share():
        return pltpu.make_async_remote_copy(
            src_ref=seam_all.at[:, my_col],
            dst_ref=seam_all.at[:, my_col],
            send_sem=share_sem.at[0],
            recv_sem=share_sem.at[1],
            device_id={"row": my_row, "col": 1 - my_col},
            device_id_type=pl.DeviceIdType.MESH,
        )

    def send_seam():
        span = count_col * windows
        shape = (2 * span, count * block)
        row = lax.broadcasted_iota(jnp.int32, shape, 0)
        way, place = (lax.div(row, span), lax.rem(row, span))
        peer = (seam - 1 + way) * count_col + lax.div(place, windows)
        rows = one_hot(
            peer * block + lax.rem(place, windows) * pair + (1 - way) * (pair - 1), shape
        )
        rows = pick(rows, flat(proj)[0])
        for way, here in ((0, below), (1, above)):
            seam_mine[way] = rows[way * span : (way + 1) * span]

            @pl.when(here)
            def _():
                seam_all[my_row, my_col] = seam_mine[way]

            @pl.when(jnp.logical_not(here))
            def _():
                relay(way).start()

    def take_seam():
        def each(owner, carry):
            @pl.when(owner != my_row)
            def _():
                seam_wait(owner)

            return carry

        lax.fori_loop(0, count_row, each, 0)
        seam_share().start()
        seam_share().wait()

    def place_seam(line):
        span = count_col * windows
        source = seam_all.reshape(count * span, channels)
        shape = (width, count * span)
        row = lax.broadcasted_iota(jnp.int32, shape, 0)
        token = jnp.where(row <= wide, row, row - width)
        for shift in range(3):
            near_token = token + shift - 1
            column = near_token + my_col * wide
            known = (near_token >= -1) & (near_token <= wide)
            known = known & (column >= 0) & (column < count_col * wide)
            moved = column + tile
            target = lax.rem(moved, tile) * span + lax.div(moved, tile) - 1
            rows = one_hot(jnp.where(known, target, -1), shape)
            for parity in range(2):
                low = 2 * parity * depth
                start = (0, depth, 3 * depth)[shift]
                first = low + (depth if shift == 0 else 0)
                size = 2 * depth if shift == 1 else depth
                shuffled[parity, line, :, start : start + size] = pick(
                    rows, source[:, first : first + size]
                )

    sends_up, sends_down = (has_up & (my_row != seam), has_down & (my_row != seam - 1))
    edges = [(parity, down) for parity in range(2) for down in (True, False)]

    def build(chunk):
        copy_r(chunk, first_step).wait_recv()
        side(chunk).start()

        def rest(step):
            @pl.when(step != first_step)
            def _():
                copy_r(chunk, step).wait_recv()

        each_peer(rest)
        side(chunk).wait()
        source = field.reshape(chunks, (count + 1) * block, channels)
        for parity in range(2):
            low = 2 * parity * depth
            even, odd = (slice(low, low + depth), slice(low + depth, low + 2 * depth))
            both = slice(low, low + 2 * depth)
            for shift, lanes, start in ((0, odd, 0), (1, both, depth), (2, even, 3 * depth)):
                rows = pick(places[shift], source[chunk, :, lanes])
                stop = start + rows.shape[1]
                for place in range(pair):
                    shuffled[parity, line_of(chunk, place), :, start:stop] = rows[
                        place * width : (place + 1) * width
                    ]

    def finish_edges():
        for parity, down in edges:
            goes, comes = (sends_down, sends_up) if down else (sends_up, sends_down)

            @pl.when(goes)
            def _():
                edge(parity, down).wait_send()

            @pl.when(comes)
            def _():
                edge(parity, down).wait_recv()

        for here, line in ((below, 0), (above, token_rows + 1)):

            @pl.when(here)
            def _():
                take_seam()
                place_seam(line)

        for way, here in ((0, below), (1, above)):

            @pl.when(jnp.logical_not(here))
            def _():
                relay(way).wait_send()

        for parity in range(2):
            for line in (0, token_rows + 1):
                shuffled[parity, line, :, 0:depth] = pick(
                    slides[0], shuffled[parity, line, :, 2 * depth : 3 * depth]
                )
                shuffled[parity, line, :, 3 * depth :] = pick(
                    slides[1], shuffled[parity, line, :, depth : 2 * depth]
                )

    def convolve_lines(source, weights, parity, other, start, stop, columns):
        if parity == 0:
            taps = ((1, -1), (0, 0), (1, 0))
        else:
            taps = ((0, 0), (1, 0), (0, 1))
        result = None
        for tap, (plane, shift) in enumerate(taps):
            cells = source[
                plane, start + shift : stop + shift, 0:columns, other * depth : (other + 3) * depth
            ].reshape((stop - start) * columns, 3 * depth)
            part = jnp.dot(cells, weights[tap], preferred_element_type=jnp.float32)
            result = part if result is None else result + part
        return result

    edge_slot = lax.broadcasted_iota(jnp.int32, (width - wide, depth), 0)
    valid = edge_slot == jnp.where(first_col, 0, width - wide - 1)

    def activate(parity, start, stop):
        for other in range(2):
            value = convolve_lines(shuffled, fk, parity, other, start, stop, width)
            value = jax.nn.gelu(value + fb_ref[...])
            for line in range(start, stop):
                cells = value[(line - start) * width : (line - start + 1) * width]
                cells = jnp.concatenate(
                    [cells[:wide], jnp.where(valid, cells[wide:], 0.0)], axis=0
                )
                if line == 0:
                    cells = jnp.where(has_up, cells, 0.0)
                if line == token_rows + 1:
                    cells = jnp.where(has_down, cells, 0.0)
                activated[parity, line, :, (other + 1) * depth : (other + 2) * depth] = (
                    cells.astype(jnp.bfloat16)
                )
                if other == 1:
                    moved = pltpu.roll(cells, 1, 0)
                    activated[parity, line, :, 0:depth] = moved.astype(jnp.bfloat16)
                else:
                    moved = pltpu.roll(cells, width - 1, 0)
                    activated[parity, line, :, 3 * depth :] = moved.astype(jnp.bfloat16)

    def store(start, stop):
        return pltpu.make_async_copy(
            out.at[pl.ds(2 * start - 2, 2 * (stop - start))],
            out_hbm.at[pl.ds(2 * start - 2, 2 * (stop - start))],
            out_sem.at[start],
        )

    def emit(start, stop):
        for parity in range(2):
            for other in range(2):
                value = convolve_lines(activated, sk, parity, other, start, stop, wide)
                value = value + sb_ref[...]
                for line in range(start, stop):
                    rows = slice((line - start) * wide, (line - start + 1) * wide)
                    for part in range(depth // LANES):
                        stage[2 * line - 2 + parity, part, pl.ds(other, wide, stride=2), :] = (
                            value[rows, part * LANES : (part + 1) * LANES]
                        )
            for line in range(start, stop):
                place = 2 * line - 2 + parity
                for part in range(depth // LANES):
                    lanes = slice(part * LANES, (part + 1) * LANES)
                    out[place, :, lanes] = stage[place, part].astype(jnp.bfloat16)
        store(start, stop).start()

    stored = []

    def finish(chunk):
        build(chunk)
        top, low = (chunk + 1, token_rows - chunk)
        if chunk == 0:
            for parity, down in edges:

                @pl.when(sends_down if down else sends_up)
                def _():
                    edge(parity, down).start()

            return
        if chunk == 1:
            finish_edges()
            activate(1, 0, 1)
            activate(0, token_rows + 1, token_rows + 2)
            activate(0, 1, 2)
            activate(1, token_rows, token_rows + 1)
        if chunk < chunks - 1:
            activate(1, top - 1, top)
            activate(0, top, top + 1)
            activate(0, low + 1, low + 2)
            activate(1, low, low + 1)
            spans = ((top - 1, top), (low + 1, low + 2))
        else:
            activate(1, top - 1, low + 1)
            activate(0, top, low + 2)
            spans = ((top - 1, low + 2),)
        for span in spans:
            emit(*span)
            stored.append(span)

    last = chunks - 1
    for chunk in range(chunks):
        across(chunk)
        if chunk < last - 1:
            send(copy_r, chunk)
            if chunk == 0:
                send_seam()
            send_chunk(chunk + 2)
            if chunk > 0:
                finish(chunk - 1)
        elif chunk < last:
            finish(chunk - 1)
            send(copy_r, chunk, [(copy, last) for copy in (copy_k, copy_q, copy_v)])
        else:
            send(copy_r, chunk, [(copy_r, chunk - 1)])
    finish(last - 1)
    finish(last)
    for chunk in (*range(last - 1), last):
        each_peer(lambda step: copy_r(chunk, step).wait_send())
    for span in stored:
        store(*span).wait()


def settle_kernel(source, target, held, sems):
    size = source.shape[0] // PIECES
    pieces = [pl.ds(piece * size, size) for piece in range(PIECES)]
    reads = [
        pltpu.make_async_copy(source.at[rows], held.at[rows], sems.at[0, piece])
        for piece, rows in enumerate(pieces)
    ]
    writes = [
        pltpu.make_async_copy(held.at[rows], target.at[rows], sems.at[1, piece])
        for piece, rows in enumerate(pieces)
    ]
    for read in reads:
        read.start()
    for read, write in zip(reads, writes):
        read.wait()
        write.start()
    for write in writes:
        write.wait()


def fused(qw, kw, vw, qi, ki, proj_weight, proj_bias, first_kernel, first_bias, second_kernel, second_bias):
    windows, tokens_win, features = qw.shape
    count_row = lax.axis_size("row")
    count_col = lax.axis_size("col")
    count = count_row * count_col
    channels = proj_weight.shape[-1]
    depth = first_kernel.shape[-1]
    taps = (first_kernel.shape[0], first_kernel.shape[1] * first_kernel.shape[2], depth)
    token_rows = tokens_win // TILE_COLS
    chunks = token_rows // LINES
    block = windows * LINES
    width = (windows + 1) * TILE_COLS
    planes = (2, token_rows + 2, width, 4 * depth)
    fine = (2 * token_rows, 2 * windows * TILE_COLS, depth)
    rows = (chunks, count, block, features)
    whole = pl.BlockSpec(memory_space=pl.ANY)
    held = pl.BlockSpec(memory_space=pltpu.VMEM)
    dma = pltpu.SemaphoreType.DMA
    result = pl.pallas_call(
        functools.partial(attention_kernel, count_row, count_col),
        out_shape=jax.ShapeDtypeStruct(fine, jnp.bfloat16),
        in_specs=[whole] * 8 + [held] * 3,
        out_specs=whole,
        scratch_shapes=[pltpu.VMEM(qw.shape, jnp.bfloat16)] * 5
        + [
            pltpu.VMEM(proj_weight.shape, jnp.bfloat16),
            pltpu.VMEM(taps, jnp.bfloat16),
            pltpu.VMEM(taps, jnp.bfloat16),
            pltpu.VMEM(qw.shape, jnp.bfloat16),
        ]
        + [pltpu.VMEM(rows, jnp.bfloat16)] * 6
        + [
            pltpu.VMEM((chunks, count, block, channels), jnp.bfloat16),
            pltpu.VMEM((chunks, count + 1, block, channels), jnp.bfloat16),
            pltpu.VMEM((2, count_col * windows, channels), jnp.bfloat16),
            pltpu.VMEM((count_row, count_col, count_col * windows, channels), jnp.bfloat16),
            pltpu.VMEM((3, LINES * width, (count + 1) * block), jnp.bfloat16),
            pltpu.VMEM((2, width, width), jnp.bfloat16),
            pltpu.VMEM(planes, jnp.bfloat16),
            pltpu.VMEM(planes, jnp.bfloat16),
            pltpu.VMEM((fine[0], depth // LANES, fine[1], LANES), jnp.float32),
            pltpu.VMEM(fine, jnp.bfloat16),
            dma((8,)),
        ]
        + [dma((chunks, count))] * 8
        + [
            dma((chunks,)),
            dma((chunks,)),
            dma((4,)),
            dma((4,)),
            dma((2,)),
            dma((count_row,)),
            dma((2,)),
            dma((token_rows + 2,)),
        ],
        compiler_params=pltpu.CompilerParams(
            collective_id=0, has_side_effects=True, vmem_limit_bytes=62 * 1024 * 1024
        ),
    )(
        qw,
        kw,
        vw,
        qi,
        ki,
        proj_weight,
        first_kernel.reshape(taps),
        second_kernel.reshape(taps),
        proj_bias.reshape(1, channels),
        first_bias.reshape(1, depth),
        second_bias.reshape(1, depth),
    )
    return pl.pallas_call(
        settle_kernel,
        out_shape=jax.ShapeDtypeStruct(fine, jnp.bfloat16),
        in_specs=[whole],
        out_specs=whole,
        scratch_shapes=[pltpu.VMEM(fine, jnp.bfloat16), dma((2, PIECES))],
    )(result)


def convolutions(
    projected, rows_dev, cols_dev, first_kernel, first_bias, second_kernel, second_bias
):
    grouped = projected.reshape(rows_dev, cols_dev, TILE_ROWS, TILE_COLS, 2, 2, CHANNELS)
    shuffled = jnp.transpose(grouped, (0, 2, 4, 1, 3, 5, 6)).reshape(
        rows_dev * TILE_ROWS * 2, cols_dev * TILE_COLS * 2, CHANNELS
    )
    activated = jax.nn.gelu(convolve(shuffled, first_kernel, first_bias)).astype(jnp.bfloat16)
    return convolve(activated, second_kernel, second_bias).astype(jnp.bfloat16)


def shards(
    query_window,
    key_window,
    value_window,
    query_index,
    key_index,
    proj_weight,
    proj_bias,
    first_kernel,
    first_bias,
    second_kernel,
    second_bias,
):
    rows_dev, cols_dev, tokens_win, features = query_window.shape
    flat = (rows_dev * cols_dev, tokens_win, features)
    owners = lax.axis_size("row") * lax.axis_size("col")
    fits = rows_dev == 1 and lax.axis_size("col") == 2 and owners == TILE_COLS
    fits = fits and tokens_win % (LINES * TILE_COLS) == 0 and tokens_win >= 4 * LINES * TILE_COLS
    if fits and cols_dev * LINES % 8 == 0 and features % LANES == 0:
        return fused(
            query_window.reshape(flat),
            key_window.reshape(flat),
            value_window.reshape(flat),
            query_index.reshape(flat),
            key_index.reshape(flat),
            proj_weight,
            proj_bias,
            first_kernel,
            first_bias,
            second_kernel,
            second_bias,
        )
    layout = (rows_dev * cols_dev, tokens_win, HEADS, HEAD_DIM)
    window_out = window_attend(
        query_window.reshape(layout), key_window.reshape(layout), value_window.reshape(layout)
    ).reshape(query_window.shape)
    count_row = lax.axis_size("row")
    count_col = lax.axis_size("col")
    owned_tokens = tokens_win // (count_row * count_col)
    moved = (
        lax.all_to_all(query_index, ("row", "col"), split_axis=2, concat_axis=0, tiled=True),
        lax.all_to_all(key_index, ("row", "col"), split_axis=2, concat_axis=0, tiled=True),
        lax.all_to_all(window_out, ("row", "col"), split_axis=2, concat_axis=0, tiled=True),
    )
    owner_shape = moved[0].shape
    across = (-1, owned_tokens, HEADS, HEAD_DIM)
    index_out = index_attend(
        moved[0].reshape(across), moved[1].reshape(across), moved[2].reshape(across)
    )
    index_rows = index_out.reshape(-1, features)
    owner_rows = (
        jnp.dot(index_rows, proj_weight, preferred_element_type=jnp.float32) + proj_bias
    ).astype(jnp.bfloat16)
    last = owner_rows.shape[-1]
    shaped = owner_rows.reshape(tuple(owner_shape[:-1]) + (last,))
    returned = lax.all_to_all(shaped, ("row", "col"), split_axis=0, concat_axis=2, tiled=True)
    projected = returned.reshape(rows_dev * cols_dev * tokens_win, last)
    return convolutions(
        projected, rows_dev, cols_dev, first_kernel, first_bias, second_kernel, second_bias
    )


def solution(mesh):
    in_specs = (
        P(("grp", "row"), "col", None, None),
        P(("grp", "row"), "col", None, None),
        P(("grp", "row"), "col", None, None),
        P(("grp", "row"), "col", None, None),
        P(("grp", "row"), "col", None, None),
        P(),
        P(),
        P(),
        P(),
        P(),
        P(),
    )
    out_specs = P(("grp", "row"), "col", None)
    return jax.shard_map(shards, mesh=mesh, in_specs=in_specs, out_specs=out_specs, check_vma=False)
```

```python
import functools
import math

import jax
import jax.numpy as jnp
from jax import lax
from jax.experimental import pallas as pl
from jax.experimental.pallas import tpu as pltpu
from jax.sharding import PartitionSpec as P

HEADS = 8
HEAD_DIM = 160
CHANNELS = 256
TILE_ROWS = 8
TILE_COLS = 16
LANES = 128
LINES = 2


def extended(value, sides, width):
    for axis, dim in sides:
        size, length = (lax.axis_size(axis), value.shape[dim])
        up = [(i, (i + 1) % size) for i in range(size - 1)]
        down = [(j, i) for i, j in up]
        last = lax.slice_in_dim(value, length - width, length, axis=dim)
        first = lax.slice_in_dim(value, 0, width, axis=dim)
        before = lax.ppermute(last, axis, up)
        after = lax.ppermute(first, axis, down)
        value = jnp.concatenate([before, value, after], axis=dim)
    return value


def softmax_rows(scores):
    highest = jnp.max(scores, axis=-1, keepdims=True)
    raised = jnp.exp(scores - highest)
    return (raised / jnp.sum(raised, axis=-1, keepdims=True)).astype(jnp.bfloat16)


def window_attend(queries, key_rows, values):
    scores = jnp.einsum(
        "blhd,bmhd->bhlm", queries, key_rows, preferred_element_type=jnp.float32
    ) / math.sqrt(HEAD_DIM)
    weights = softmax_rows(scores)
    return jnp.einsum(
        "bhlm,bmhd->blhd", weights, values, preferred_element_type=jnp.float32
    ).astype(jnp.bfloat16)


def index_attend(queries, key_rows, values):
    scores = jnp.einsum(
        "lbhd,mbhd->bhlm", queries, key_rows, preferred_element_type=jnp.float32
    ) / math.sqrt(HEAD_DIM)
    weights = softmax_rows(scores)
    return jnp.einsum(
        "bhlm,mbhd->lbhd", weights, values, preferred_element_type=jnp.float32
    ).astype(jnp.bfloat16)


def convolve(image, kernel, bias):
    height, breadth, depth = image.shape
    padded = extended(image, (("row", 0), ("col", 1)), 1)
    total = jnp.zeros((height * breadth, kernel.shape[-1]), jnp.float32)
    for row_shift in range(3):
        for col_shift in range(3):
            cells = padded[row_shift : row_shift + height, col_shift : col_shift + breadth].reshape(
                -1, depth
            )
            total = total + jnp.dot(
                cells, kernel[row_shift, col_shift], preferred_element_type=jnp.float32
            )
    return (total + bias).reshape(height, breadth, -1)


def attend_heads(queries, key_part, value_part, same):
    rows, features = queries.shape
    head_dim = features // HEADS
    factor = math.log2(math.e) / math.sqrt(head_dim)
    blocks = [None] * (features // LANES)
    for head in range(HEADS):
        low, high = (head * head_dim, (head + 1) * head_dim)
        start, stop = (low // LANES * LANES, -(-high // LANES) * LANES)
        lane = lax.broadcasted_iota(jnp.int32, (rows, stop - start), 1) + start
        inside = (lane >= low) & (lane < high)
        part = queries[:, start:stop]
        part = jnp.where(inside, part, jnp.zeros_like(part))
        scores = lax.dot_general(
            part,
            key_part(start, stop),
            (((1,), (1,)), ((), ())),
            preferred_element_type=jnp.float32,
        )
        if same is not None:
            scores = jnp.where(same, scores, -1e30)
        highest = jnp.max(scores, axis=-1, keepdims=True)
        raised = jnp.exp2((scores - highest) * factor)
        weights = (raised * (1.0 / jnp.sum(raised, axis=-1, keepdims=True))).astype(jnp.bfloat16)
        mixed = jnp.dot(weights, value_part(start, stop), preferred_element_type=jnp.float32)
        mixed = jnp.where(inside, mixed, 0.0)
        for block in range(start // LANES, stop // LANES):
            piece = mixed[:, block * LANES - start : (block + 1) * LANES - start]
            blocks[block] = piece if blocks[block] is None else blocks[block] + piece
    return jnp.concatenate(blocks, axis=1).astype(jnp.bfloat16)


def one_hot(target, shape):
    return (lax.broadcasted_iota(jnp.int32, shape, 1) == target).astype(jnp.bfloat16)


def pick(rows, source):
    return jnp.dot(rows, source, preferred_element_type=jnp.float32).astype(jnp.bfloat16)


def attention_kernel(
    count_row,
    count_col,
    qw_hbm,
    kw_hbm,
    vw_hbm,
    qi_hbm,
    ki_hbm,
    pw_hbm,
    fk_hbm,
    sk_hbm,
    pb_ref,
    fb_ref,
    sb_ref,
    out,
    qw,
    kw,
    vw,
    qi,
    ki,
    pw,
    fk,
    sk,
    window_out,
    order,
    k_mine,
    q_mine,
    v_mine,
    k_all,
    q_all,
    v_all,
    proj,
    field,
    seam_mine,
    seam_all,
    places,
    slides,
    shuffled,
    activated,
    stage,
    load_sem,
    ki_sem,
    qi_sem,
    k_send,
    k_recv,
    q_send,
    q_recv,
    v_send,
    v_recv,
    r_send,
    r_recv,
    side_send,
    side_recv,
    edge_send,
    edge_recv,
    seam_send,
    seam_recv,
    share_sem,
):
    count = count_row * count_col
    half = count // 2
    windows, tokens_win, features = qw.shape
    tile = TILE_COLS
    token_rows = tokens_win // tile
    chunks, _, block, channels = proj.shape
    pair = block // windows
    wide = windows * tile
    width = shuffled.shape[2]
    depth = fk.shape[-1]
    my_row, my_col = (lax.axis_index("row"), lax.axis_index("col"))
    me = my_row * count_col + my_col
    my_half, my_place = (me // half, lax.rem(me, half))

    def peer_of(step):
        across = (1 - my_half) * half + lax.rem(my_place + step, half)
        beside = my_half * half + lax.rem(my_place + step + 1, half)
        return jnp.where(step < half, across, beside)

    def device(peer):
        return {"row": peer // count_col, "col": lax.rem(peer, count_col)}

    def each_peer(body):
        def step(index, carry):
            body(index)
            return carry

        lax.fori_loop(0, count - 1, step, 0)

    barrier = pltpu.get_barrier_semaphore()

    def greet(step):
        pl.semaphore_signal(
            barrier,
            inc=1,
            device_id=device(peer_of(step)),
            device_id_type=pl.DeviceIdType.MESH,
        )

    each_peer(greet)

    def line_at(chunk, place):
        return chunk if place == 0 else token_rows - 1 - chunk

    def load_lines(source, target, sems, chunk):
        return [
            pltpu.make_async_copy(
                source.at[:, pl.ds(line_at(chunk, place) * tile, tile), :],
                target.at[chunk, place],
                sems.at[chunk, place],
            )
            for place in range(pair)
        ]

    pairs = ((ki_hbm, ki, ki_sem), (qi_hbm, qi, qi_sem))
    lines = [[load_lines(*kind, chunk) for kind in pairs] for chunk in range(chunks)]
    loads = [
        pltpu.make_async_copy(source, target, load_sem.at[place])
        for place, (source, target) in enumerate(
            (
                (qw_hbm, qw),
                (kw_hbm, kw),
                (vw_hbm, vw),
                (pw_hbm, pw),
                (fk_hbm, fk),
                (sk_hbm, sk),
            )
        )
    ]
    for kinds in lines:
        for kind in kinds:
            for load in kind:
                load.start()
    for load in loads:
        load.start()

    def sender(source, target, sems):
        def copy(chunk, step):
            peer = peer_of(step)
            return pltpu.make_async_remote_copy(
                src_ref=source.at[chunk, peer],
                dst_ref=target.at[chunk, me],
                send_sem=sems[0].at[chunk, step],
                recv_sem=sems[1].at[chunk, step],
                device_id=device(peer),
                device_id_type=pl.DeviceIdType.MESH,
            )

        return copy

    copy_k = sender(k_mine, k_all, (k_send, k_recv))
    copy_q = sender(q_mine, q_all, (q_send, q_recv))
    copy_v = sender(v_mine, v_all, (v_send, v_recv))
    copy_r = sender(proj, field, (r_send, r_recv))

    def flat(ref):
        return ref.reshape(chunks, count * block, ref.shape[-1])

    square = (count * block, count * block)
    row = lax.broadcasted_iota(jnp.int32, square, 0)
    order[...] = one_hot(
        lax.rem(row, pair) * wide + lax.div(lax.rem(row, block), pair) * tile + lax.div(row, block),
        square,
    )

    def arrange(source, mine, everyone, chunk):
        rows = source.reshape(chunks, count * block, features)[chunk]
        flat(mine)[chunk] = pick(order[...], rows)
        everyone[chunk, me] = mine[chunk, me]

    def arrange_loaded(chunk, kind):
        for load in lines[chunk][kind]:
            load.wait()
        arrange((ki, qi)[kind], (k_mine, q_mine)[kind], (k_all, q_all)[kind], chunk)

    def send(copy, chunk, before=None):
        def step(index):
            if before is not None:
                for earlier, place in before:
                    earlier(place, index).wait_send()
            copy(chunk, index).start()

        each_peer(step)

    for line in (0, token_rows + 1):
        for parity in range(2):
            shuffled[parity, line] = jnp.zeros(shuffled.shape[2:], jnp.bfloat16)
    arrange_loaded(0, 0)
    pl.semaphore_wait(barrier, count - 1)
    send(copy_k, 0)
    arrange_loaded(0, 1)
    send(copy_q, 0)
    for chunk in range(1, chunks):
        arrange_loaded(chunk, 0)
        arrange_loaded(chunk, 1)

    for load in loads:
        load.wait()

    def within(window, carry):
        rows = attend_heads(
            qw[window],
            lambda start, stop: kw[window, :, start:stop],
            lambda start, stop: vw[window, :, start:stop],
            None,
        )
        for chunk in range(chunks):
            for place in range(pair):
                line = line_at(chunk, place)
                window_out[chunk, place, window] = rows[line * tile : (line + 1) * tile]
        return carry

    lax.fori_loop(0, windows, within, 0)

    def next_values(chunk, carry):
        arrange(window_out, v_mine, v_all, chunk)
        return carry

    lax.fori_loop(0, chunks, next_values, 0)
    send(copy_v, 0)

    def send_chunk(chunk):
        for copy in (copy_k, copy_q, copy_v):
            send(copy, chunk, [(copy, chunk - 1)])

    send_chunk(1)

    same = lax.rem(lax.broadcasted_iota(jnp.int32, square, 0), pair) == lax.rem(
        lax.broadcasted_iota(jnp.int32, square, 1), pair
    )

    def across(chunk):
        for copy in (copy_k, copy_q, copy_v):
            each_peer(lambda step: copy(chunk, step).wait_recv())
        mixed = attend_heads(
            flat(q_all)[chunk],
            lambda start, stop: flat(k_all)[chunk, :, start:stop],
            lambda start, stop: flat(v_all)[chunk, :, start:stop],
            same,
        )
        rows = jnp.dot(mixed, pw[...], preferred_element_type=jnp.float32) + pb_ref[...]
        flat(proj)[chunk] = rows.astype(jnp.bfloat16)
        field[chunk, me] = proj[chunk, me]

    has_up, has_down = (my_row > 0, my_row < count_row - 1)
    first_col = my_col == 0

    shape = (pair * width, (count + 1) * block)
    row = lax.broadcasted_iota(jnp.int32, shape, 0)
    slot, place = (lax.rem(row, width), lax.div(row, width))
    token = jnp.where(slot <= wide, slot, slot - width)

    def source_row(column):
        inside = (column >= 0) & (column < wide)
        own = lax.rem(column + tile, tile) * block + lax.div(column + tile, tile) * pair - pair
        right = jnp.where((column == wide) & first_col, count * block, -token_rows)
        left = jnp.where(
            (column == -1) & (my_col > 0), count * block + (windows - 1) * pair, right
        )
        return jnp.where(inside, own, left) + place

    for shift in range(3):
        places[shift] = one_hot(source_row(token + shift - 1), shape)
    shape = (width, width)
    row = lax.broadcasted_iota(jnp.int32, shape, 0)
    for way in range(2):
        slides[way] = one_hot(lax.rem(row + width + 2 * way - 1, width), shape)

    def line_of(chunk, place):
        return chunk + 1 if place == 0 else token_rows - chunk

    near = jnp.where(first_col, count - 1, 0)
    turn = lax.rem(my_place - lax.rem(near, half) + half, half)
    first_step = jnp.where(
        near // half == my_half, half + lax.rem(turn - 1 + half, half), turn
    )

    def side(chunk):
        return pltpu.make_async_remote_copy(
            src_ref=field.at[chunk, near],
            dst_ref=field.at[chunk, count],
            send_sem=side_send.at[chunk],
            recv_sem=side_recv.at[chunk],
            device_id={"row": my_row, "col": 1 - my_col},
            device_id_type=pl.DeviceIdType.MESH,
        )

    def edge(parity, down):
        lanes = pl.ds(depth, 2 * depth)
        source, target = (token_rows, 0) if down else (1, token_rows + 1)
        place = 2 * parity + (1 if down else 0)
        return pltpu.make_async_remote_copy(
            src_ref=shuffled.at[parity, source, :, lanes],
            dst_ref=shuffled.at[parity, target, :, lanes],
            send_sem=edge_send.at[place],
            recv_sem=edge_recv.at[place],
            device_id={"row": my_row + (1 if down else -1), "col": my_col},
            device_id_type=pl.DeviceIdType.MESH,
        )

    seam = count_row // 2
    above, below = (my_row == seam - 1, my_row == seam)

    def relay(way):
        return pltpu.make_async_remote_copy(
            src_ref=seam_mine.at[way],
            dst_ref=seam_all.at[my_row, my_col],
            send_sem=seam_send.at[way],
            recv_sem=seam_recv.at[my_row],
            device_id={"row": jnp.where(way == 0, seam, seam - 1), "col": my_col},
            device_id_type=pl.DeviceIdType.MESH,
        )

    def seam_wait(owner):
        pltpu.make_async_remote_copy(
            src_ref=seam_mine.at[0],
            dst_ref=seam_all.at[owner, my_col],
            send_sem=seam_send.at[0],
            recv_sem=seam_recv.at[owner],
            device_id={"row": my_row, "col": 1 - my_col},
            device_id_type=pl.DeviceIdType.MESH,
        ).wait_recv()

    def seam_share():
        return pltpu.make_async_remote_copy(
            src_ref=seam_all.at[:, my_col],
            dst_ref=seam_all.at[:, my_col],
            send_sem=share_sem.at[0],
            recv_sem=share_sem.at[1],
            device_id={"row": my_row, "col": 1 - my_col},
            device_id_type=pl.DeviceIdType.MESH,
        )

    def send_seam():
        span = count_col * windows
        shape = (2 * span, count * block)
        row = lax.broadcasted_iota(jnp.int32, shape, 0)
        way, place = (lax.div(row, span), lax.rem(row, span))
        peer = (seam - 1 + way) * count_col + lax.div(place, windows)
        rows = one_hot(
            peer * block + lax.rem(place, windows) * pair + (1 - way) * (pair - 1), shape
        )
        rows = pick(rows, flat(proj)[0])
        for way, here in ((0, below), (1, above)):
            seam_mine[way] = rows[way * span : (way + 1) * span]

            @pl.when(here)
            def _():
                seam_all[my_row, my_col] = seam_mine[way]

            @pl.when(jnp.logical_not(here))
            def _():
                relay(way).start()

    def take_seam():
        def each(owner, carry):
            @pl.when(owner != my_row)
            def _():
                seam_wait(owner)

            return carry

        lax.fori_loop(0, count_row, each, 0)
        seam_share().start()
        seam_share().wait()

    def place_seam(line):
        span = count_col * windows
        source = seam_all.reshape(count * span, channels)
        shape = (width, count * span)
        row = lax.broadcasted_iota(jnp.int32, shape, 0)
        token = jnp.where(row <= wide, row, row - width)
        for shift in range(3):
            near_token = token + shift - 1
            column = near_token + my_col * wide
            known = (near_token >= -1) & (near_token <= wide)
            known = known & (column >= 0) & (column < count_col * wide)
            moved = column + tile
            target = lax.rem(moved, tile) * span + lax.div(moved, tile) - 1
            rows = one_hot(jnp.where(known, target, -1), shape)
            for parity in range(2):
                low = 2 * parity * depth
                start = (0, depth, 3 * depth)[shift]
                first = low + (depth if shift == 0 else 0)
                size = 2 * depth if shift == 1 else depth
                shuffled[parity, line, :, start : start + size] = pick(
                    rows, source[:, first : first + size]
                )

    sends_up, sends_down = (has_up & (my_row != seam), has_down & (my_row != seam - 1))
    edges = [(parity, down) for parity in range(2) for down in (True, False)]

    def build(chunk):
        copy_r(chunk, first_step).wait_recv()
        side(chunk).start()

        def rest(step):
            @pl.when(step != first_step)
            def _():
                copy_r(chunk, step).wait_recv()

        each_peer(rest)
        side(chunk).wait()
        source = field.reshape(chunks, (count + 1) * block, channels)
        for parity in range(2):
            low = 2 * parity * depth
            even, odd = (slice(low, low + depth), slice(low + depth, low + 2 * depth))
            both = slice(low, low + 2 * depth)
            for shift, lanes, start in ((0, odd, 0), (1, both, depth), (2, even, 3 * depth)):
                rows = pick(places[shift], source[chunk, :, lanes])
                stop = start + rows.shape[1]
                for place in range(pair):
                    shuffled[parity, line_of(chunk, place), :, start:stop] = rows[
                        place * width : (place + 1) * width
                    ]

    def finish_edges():
        for parity, down in edges:
            goes, comes = (sends_down, sends_up) if down else (sends_up, sends_down)

            @pl.when(goes)
            def _():
                edge(parity, down).wait_send()

            @pl.when(comes)
            def _():
                edge(parity, down).wait_recv()

        for here, line in ((below, 0), (above, token_rows + 1)):

            @pl.when(here)
            def _():
                take_seam()
                place_seam(line)

        for way, here in ((0, below), (1, above)):

            @pl.when(jnp.logical_not(here))
            def _():
                relay(way).wait_send()

        for parity in range(2):
            for line in (0, token_rows + 1):
                shuffled[parity, line, :, 0:depth] = pick(
                    slides[0], shuffled[parity, line, :, 2 * depth : 3 * depth]
                )
                shuffled[parity, line, :, 3 * depth :] = pick(
                    slides[1], shuffled[parity, line, :, depth : 2 * depth]
                )

    def convolve_lines(source, weights, parity, other, start, stop, columns):
        if parity == 0:
            taps = ((1, -1), (0, 0), (1, 0))
        else:
            taps = ((0, 0), (1, 0), (0, 1))
        cells = [
            source[
                plane, start + shift : stop + shift, 0:columns, other * depth : (other + 3) * depth
            ].reshape((stop - start) * columns, 3 * depth)
            for plane, shift in taps
        ]
        return jnp.dot(
            jnp.concatenate(cells, axis=1),
            weights.reshape(weights.shape[0] * weights.shape[1], depth)[...],
            preferred_element_type=jnp.float32,
        )

    edge_slot = lax.broadcasted_iota(jnp.int32, (width - wide, depth), 0)
    valid = edge_slot == jnp.where(first_col, 0, width - wide - 1)

    def activate(parity, start, stop):
        for other in range(2):
            value = convolve_lines(shuffled, fk, parity, other, start, stop, width)
            value = jax.nn.gelu(value + fb_ref[...])
            for line in range(start, stop):
                cells = value[(line - start) * width : (line - start + 1) * width]
                cells = jnp.concatenate(
                    [cells[:wide], jnp.where(valid, cells[wide:], 0.0)], axis=0
                )
                if line == 0:
                    cells = jnp.where(has_up, cells, 0.0)
                if line == token_rows + 1:
                    cells = jnp.where(has_down, cells, 0.0)
                activated[parity, line, :, (other + 1) * depth : (other + 2) * depth] = (
                    cells.astype(jnp.bfloat16)
                )
                if other == 1:
                    moved = pltpu.roll(cells, 1, 0)
                    activated[parity, line, :, 0:depth] = moved.astype(jnp.bfloat16)
                else:
                    moved = pltpu.roll(cells, width - 1, 0)
                    activated[parity, line, :, 3 * depth :] = moved.astype(jnp.bfloat16)

    def emit(start, stop):
        for parity in range(2):
            for other in range(2):
                value = convolve_lines(activated, sk, parity, other, start, stop, wide)
                value = value + sb_ref[...]
                for line in range(start, stop):
                    rows = slice((line - start) * wide, (line - start + 1) * wide)
                    for part in range(depth // LANES):
                        stage[2 * line - 2 + parity, part, pl.ds(other, wide, stride=2), :] = (
                            value[rows, part * LANES : (part + 1) * LANES]
                        )
            for line in range(start, stop):
                place = 2 * line - 2 + parity
                for part in range(depth // LANES):
                    lanes = slice(part * LANES, (part + 1) * LANES)
                    out[place, :, lanes] = stage[place, part].astype(jnp.bfloat16)

    def finish(chunk):
        build(chunk)
        top, low = (chunk + 1, token_rows - chunk)
        if chunk == 0:
            for parity, down in edges:

                @pl.when(sends_down if down else sends_up)
                def _():
                    edge(parity, down).start()

            return
        if chunk == 1:
            finish_edges()
            activate(1, 0, 1)
            activate(0, token_rows + 1, token_rows + 2)
            activate(0, 1, 2)
            activate(1, token_rows, token_rows + 1)
        if chunk < chunks - 1:
            activate(1, top - 1, top)
            activate(0, top, top + 1)
            activate(0, low + 1, low + 2)
            activate(1, low, low + 1)
            spans = ((top - 1, top), (low + 1, low + 2))
        else:
            activate(1, top - 1, low + 1)
            activate(0, top, low + 2)
            spans = ((top - 1, low + 2),)
        for span in spans:
            emit(*span)

    last = chunks - 1
    for chunk in range(chunks):
        across(chunk)
        if chunk < last - 1:
            send(copy_r, chunk)
            if chunk == 0:
                send_seam()
            send_chunk(chunk + 2)
            if chunk > 0:
                finish(chunk - 1)
        elif chunk < last:
            finish(chunk - 1)
            send(copy_r, chunk, [(copy, last) for copy in (copy_k, copy_q, copy_v)])
        else:
            send(copy_r, chunk, [(copy_r, chunk - 1)])
    finish(last - 1)
    finish(last)
    for chunk in (*range(last - 1), last):
        each_peer(lambda step: copy_r(chunk, step).wait_send())


def fused(qw, kw, vw, qi, ki, proj_weight, proj_bias, first_kernel, first_bias, second_kernel, second_bias):
    windows, tokens_win, features = qw.shape
    count_row = lax.axis_size("row")
    count_col = lax.axis_size("col")
    count = count_row * count_col
    channels = proj_weight.shape[-1]
    depth = first_kernel.shape[-1]
    taps = (first_kernel.shape[0], first_kernel.shape[1] * first_kernel.shape[2], depth)
    token_rows = tokens_win // TILE_COLS
    chunks = token_rows // LINES
    block = windows * LINES
    width = (windows + 1) * TILE_COLS
    planes = (2, token_rows + 2, width, 4 * depth)
    fine = (2 * token_rows, 2 * windows * TILE_COLS, depth)
    rows = (chunks, count, block, features)
    lines = (chunks, LINES, windows, TILE_COLS, features)
    whole = pl.BlockSpec(memory_space=pl.ANY)
    held = pl.BlockSpec(memory_space=pltpu.VMEM)
    dma = pltpu.SemaphoreType.DMA
    return pl.pallas_call(
        functools.partial(attention_kernel, count_row, count_col),
        out_shape=pltpu.VMEM(fine, jnp.bfloat16),
        in_specs=[whole] * 8 + [held] * 3,
        out_specs=held,
        scratch_shapes=[pltpu.VMEM(qw.shape, jnp.bfloat16)] * 3
        + [pltpu.VMEM(lines, jnp.bfloat16)] * 2
        + [
            pltpu.VMEM(proj_weight.shape, jnp.bfloat16),
            pltpu.VMEM(taps, jnp.bfloat16),
            pltpu.VMEM(taps, jnp.bfloat16),
            pltpu.VMEM(lines, jnp.bfloat16),
            pltpu.VMEM((count * block, count * block), jnp.bfloat16),
        ]
        + [pltpu.VMEM(rows, jnp.bfloat16)] * 6
        + [
            pltpu.VMEM((chunks, count, block, channels), jnp.bfloat16),
            pltpu.VMEM((chunks, count + 1, block, channels), jnp.bfloat16),
            pltpu.VMEM((2, count_col * windows, channels), jnp.bfloat16),
            pltpu.VMEM((count_row, count_col, count_col * windows, channels), jnp.bfloat16),
            pltpu.VMEM((3, LINES * width, (count + 1) * block), jnp.bfloat16),
            pltpu.VMEM((2, width, width), jnp.bfloat16),
            pltpu.VMEM(planes, jnp.bfloat16),
            pltpu.VMEM(planes, jnp.bfloat16),
            pltpu.VMEM((fine[0], depth // LANES, fine[1], LANES), jnp.float32),
            dma((6,)),
            dma((chunks, LINES)),
            dma((chunks, LINES)),
        ]
        + [dma((chunks, count))] * 8
        + [
            dma((chunks,)),
            dma((chunks,)),
            dma((4,)),
            dma((4,)),
            dma((2,)),
            dma((count_row,)),
            dma((2,)),
        ],
        compiler_params=pltpu.CompilerParams(
            collective_id=0, has_side_effects=True, vmem_limit_bytes=60 * 1024 * 1024
        ),
    )(
        qw,
        kw,
        vw,
        qi,
        ki,
        proj_weight,
        first_kernel.reshape(taps),
        second_kernel.reshape(taps),
        proj_bias.reshape(1, channels),
        first_bias.reshape(1, depth),
        second_bias.reshape(1, depth),
    )


def convolutions(
    projected, rows_dev, cols_dev, first_kernel, first_bias, second_kernel, second_bias
):
    grouped = projected.reshape(rows_dev, cols_dev, TILE_ROWS, TILE_COLS, 2, 2, CHANNELS)
    shuffled = jnp.transpose(grouped, (0, 2, 4, 1, 3, 5, 6)).reshape(
        rows_dev * TILE_ROWS * 2, cols_dev * TILE_COLS * 2, CHANNELS
    )
    activated = jax.nn.gelu(convolve(shuffled, first_kernel, first_bias)).astype(jnp.bfloat16)
    return convolve(activated, second_kernel, second_bias).astype(jnp.bfloat16)


def shards(
    query_window,
    key_window,
    value_window,
    query_index,
    key_index,
    proj_weight,
    proj_bias,
    first_kernel,
    first_bias,
    second_kernel,
    second_bias,
):
    rows_dev, cols_dev, tokens_win, features = query_window.shape
    flat = (rows_dev * cols_dev, tokens_win, features)
    owners = lax.axis_size("row") * lax.axis_size("col")
    fits = rows_dev == 1 and lax.axis_size("col") == 2 and owners == TILE_COLS
    fits = fits and tokens_win % (LINES * TILE_COLS) == 0 and tokens_win >= 4 * LINES * TILE_COLS
    if fits and cols_dev * LINES % 8 == 0 and features % LANES == 0:
        return fused(
            query_window.reshape(flat),
            key_window.reshape(flat),
            value_window.reshape(flat),
            query_index.reshape(flat),
            key_index.reshape(flat),
            proj_weight,
            proj_bias,
            first_kernel,
            first_bias,
            second_kernel,
            second_bias,
        )
    layout = (rows_dev * cols_dev, tokens_win, HEADS, HEAD_DIM)
    window_out = window_attend(
        query_window.reshape(layout), key_window.reshape(layout), value_window.reshape(layout)
    ).reshape(query_window.shape)
    count_row = lax.axis_size("row")
    count_col = lax.axis_size("col")
    owned_tokens = tokens_win // (count_row * count_col)
    moved = (
        lax.all_to_all(query_index, ("row", "col"), split_axis=2, concat_axis=0, tiled=True),
        lax.all_to_all(key_index, ("row", "col"), split_axis=2, concat_axis=0, tiled=True),
        lax.all_to_all(window_out, ("row", "col"), split_axis=2, concat_axis=0, tiled=True),
    )
    owner_shape = moved[0].shape
    across = (-1, owned_tokens, HEADS, HEAD_DIM)
    index_out = index_attend(
        moved[0].reshape(across), moved[1].reshape(across), moved[2].reshape(across)
    )
    index_rows = index_out.reshape(-1, features)
    owner_rows = (
        jnp.dot(index_rows, proj_weight, preferred_element_type=jnp.float32) + proj_bias
    ).astype(jnp.bfloat16)
    last = owner_rows.shape[-1]
    shaped = owner_rows.reshape(tuple(owner_shape[:-1]) + (last,))
    returned = lax.all_to_all(shaped, ("row", "col"), split_axis=0, concat_axis=2, tiled=True)
    projected = returned.reshape(rows_dev * cols_dev * tokens_win, last)
    return convolutions(
        projected, rows_dev, cols_dev, first_kernel, first_bias, second_kernel, second_bias
    )


def solution(mesh):
    in_specs = (
        P(("grp", "row"), "col", None, None),
        P(("grp", "row"), "col", None, None),
        P(("grp", "row"), "col", None, None),
        P(("grp", "row"), "col", None, None),
        P(("grp", "row"), "col", None, None),
        P(),
        P(),
        P(),
        P(),
        P(),
        P(),
    )
    out_specs = P(("grp", "row"), "col", None)
    return jax.shard_map(shards, mesh=mesh, in_specs=in_specs, out_specs=out_specs, check_vma=False)
```

```python
import functools
import math

import jax
import jax.numpy as jnp
from jax import lax
from jax.experimental import pallas as pl
from jax.experimental.pallas import tpu as pltpu
from jax.sharding import PartitionSpec as P

HEADS = 8
HEAD_DIM = 160
CHANNELS = 256
TILE_ROWS = 8
TILE_COLS = 16
LANES = 128
LINES = 2


def extended(value, sides, width):
    for axis, dim in sides:
        size, length = (lax.axis_size(axis), value.shape[dim])
        up = [(i, (i + 1) % size) for i in range(size - 1)]
        down = [(j, i) for i, j in up]
        last = lax.slice_in_dim(value, length - width, length, axis=dim)
        first = lax.slice_in_dim(value, 0, width, axis=dim)
        before = lax.ppermute(last, axis, up)
        after = lax.ppermute(first, axis, down)
        value = jnp.concatenate([before, value, after], axis=dim)
    return value


def softmax_rows(scores):
    highest = jnp.max(scores, axis=-1, keepdims=True)
    raised = jnp.exp(scores - highest)
    return (raised / jnp.sum(raised, axis=-1, keepdims=True)).astype(jnp.bfloat16)


def window_attend(queries, key_rows, values):
    scores = jnp.einsum(
        "blhd,bmhd->bhlm", queries, key_rows, preferred_element_type=jnp.float32
    ) / math.sqrt(HEAD_DIM)
    weights = softmax_rows(scores)
    return jnp.einsum(
        "bhlm,bmhd->blhd", weights, values, preferred_element_type=jnp.float32
    ).astype(jnp.bfloat16)


def index_attend(queries, key_rows, values):
    scores = jnp.einsum(
        "lbhd,mbhd->bhlm", queries, key_rows, preferred_element_type=jnp.float32
    ) / math.sqrt(HEAD_DIM)
    weights = softmax_rows(scores)
    return jnp.einsum(
        "bhlm,mbhd->lbhd", weights, values, preferred_element_type=jnp.float32
    ).astype(jnp.bfloat16)


def convolve(image, kernel, bias):
    height, breadth, depth = image.shape
    padded = extended(image, (("row", 0), ("col", 1)), 1)
    total = jnp.zeros((height * breadth, kernel.shape[-1]), jnp.float32)
    for row_shift in range(3):
        for col_shift in range(3):
            cells = padded[row_shift : row_shift + height, col_shift : col_shift + breadth].reshape(
                -1, depth
            )
            total = total + jnp.dot(
                cells, kernel[row_shift, col_shift], preferred_element_type=jnp.float32
            )
    return (total + bias).reshape(height, breadth, -1)


def attend_heads(queries, key_part, value_part, same):
    rows, features = queries.shape
    head_dim = features // HEADS
    factor = math.log2(math.e) / math.sqrt(head_dim)
    blocks = [None] * (features // LANES)
    for head in range(HEADS):
        low, high = (head * head_dim, (head + 1) * head_dim)
        start, stop = (low // LANES * LANES, -(-high // LANES) * LANES)
        lane = lax.broadcasted_iota(jnp.int32, (rows, stop - start), 1) + start
        inside = (lane >= low) & (lane < high)
        part = queries[:, start:stop]
        part = jnp.where(inside, part, jnp.zeros_like(part))
        scores = lax.dot_general(
            part,
            key_part(start, stop),
            (((1,), (1,)), ((), ())),
            preferred_element_type=jnp.float32,
        )
        if same is not None:
            scores = jnp.where(same, scores, -1e30)
        highest = jnp.max(scores, axis=-1, keepdims=True)
        raised = jnp.exp2((scores - highest) * factor)
        weights = (raised * (1.0 / jnp.sum(raised, axis=-1, keepdims=True))).astype(jnp.bfloat16)
        mixed = jnp.dot(weights, value_part(start, stop), preferred_element_type=jnp.float32)
        mixed = jnp.where(inside, mixed, 0.0)
        for block in range(start // LANES, stop // LANES):
            piece = mixed[:, block * LANES - start : (block + 1) * LANES - start]
            blocks[block] = piece if blocks[block] is None else blocks[block] + piece
    return jnp.concatenate(blocks, axis=1).astype(jnp.bfloat16)


def one_hot(target, shape):
    return (lax.broadcasted_iota(jnp.int32, shape, 1) == target).astype(jnp.bfloat16)


def pick(rows, source):
    return jnp.dot(rows, source, preferred_element_type=jnp.float32).astype(jnp.bfloat16)


def attention_kernel(
    count_row,
    count_col,
    qw_hbm,
    kw_hbm,
    vw_hbm,
    qi_hbm,
    ki_hbm,
    pw_hbm,
    fk_hbm,
    sk_hbm,
    pb_hbm,
    fb_hbm,
    sb_hbm,
    out,
    qw,
    kw,
    vw,
    qi,
    ki,
    pw,
    fk,
    sk,
    pb,
    fb,
    sb,
    window_out,
    order,
    k_mine,
    q_mine,
    v_mine,
    k_all,
    q_all,
    v_all,
    proj,
    field,
    seam_mine,
    seam_all,
    places,
    slides,
    shuffled,
    activated,
    stage,
    load_sem,
    ki_sem,
    qi_sem,
    k_send,
    k_recv,
    q_send,
    q_recv,
    v_send,
    v_recv,
    r_send,
    r_recv,
    side_send,
    side_recv,
    edge_send,
    edge_recv,
    seam_send,
    seam_recv,
    share_sem,
):
    count = count_row * count_col
    half = count // 2
    windows, tokens_win, features = qw.shape
    tile = TILE_COLS
    token_rows = tokens_win // tile
    chunks, _, block, channels = proj.shape
    pair = block // windows
    wide = windows * tile
    width = shuffled.shape[2]
    depth = fk.shape[-1]
    my_row, my_col = (lax.axis_index("row"), lax.axis_index("col"))
    me = my_row * count_col + my_col
    my_half, my_place = (me // half, lax.rem(me, half))

    def peer_of(step):
        across = (1 - my_half) * half + lax.rem(my_place + step, half)
        beside = my_half * half + lax.rem(my_place + step + 1, half)
        return jnp.where(step < half, across, beside)

    def device(peer):
        return {"row": peer // count_col, "col": lax.rem(peer, count_col)}

    def each_peer(body):
        def step(index, carry):
            body(index)
            return carry

        lax.fori_loop(0, count - 1, step, 0)

    def line_at(chunk, place):
        return chunk if place == 0 else token_rows - 1 - chunk

    def load_lines(source, target, sems, chunk):
        return [
            pltpu.make_async_copy(
                source.at[:, pl.ds(line_at(chunk, place) * tile, tile), :],
                target.at[chunk, place],
                sems.at[chunk, place],
            )
            for place in range(pair)
        ]

    pairs = ((ki_hbm, ki, ki_sem), (qi_hbm, qi, qi_sem))
    lines = [[load_lines(*kind, chunk) for kind in pairs] for chunk in range(chunks)]
    loads = [
        pltpu.make_async_copy(source, target, load_sem.at[place])
        for place, (source, target) in enumerate(
            (
                (qw_hbm, qw),
                (kw_hbm, kw),
                (vw_hbm, vw),
                (pw_hbm, pw),
                (fk_hbm, fk),
                (sk_hbm, sk),
                (pb_hbm, pb),
                (fb_hbm, fb),
                (sb_hbm, sb),
            )
        )
    ]
    for load in lines[0][0]:
        load.start()

    barrier = pltpu.get_barrier_semaphore()

    def greet(step):
        pl.semaphore_signal(
            barrier,
            inc=1,
            device_id=device(peer_of(step)),
            device_id_type=pl.DeviceIdType.MESH,
        )

    each_peer(greet)

    def sender(source, target, sems):
        def copy(chunk, step):
            peer = peer_of(step)
            return pltpu.make_async_remote_copy(
                src_ref=source.at[chunk, peer],
                dst_ref=target.at[chunk, me],
                send_sem=sems[0].at[chunk, step],
                recv_sem=sems[1].at[chunk, step],
                device_id=device(peer),
                device_id_type=pl.DeviceIdType.MESH,
            )

        return copy

    copy_k = sender(k_mine, k_all, (k_send, k_recv))
    copy_q = sender(q_mine, q_all, (q_send, q_recv))
    copy_v = sender(v_mine, v_all, (v_send, v_recv))
    copy_r = sender(proj, field, (r_send, r_recv))

    def flat(ref):
        return ref.reshape(chunks, count * block, ref.shape[-1])

    square = (count * block, count * block)
    row = lax.broadcasted_iota(jnp.int32, square, 0)
    order[...] = one_hot(
        lax.rem(row, pair) * wide + lax.div(lax.rem(row, block), pair) * tile + lax.div(row, block),
        square,
    )

    def arrange(source, mine, everyone, chunk):
        rows = source.reshape(chunks, count * block, features)[chunk]
        flat(mine)[chunk] = pick(order[...], rows)
        everyone[chunk, me] = mine[chunk, me]

    def arrange_loaded(chunk, kind):
        for load in lines[chunk][kind]:
            load.wait()
        arrange((ki, qi)[kind], (k_mine, q_mine)[kind], (k_all, q_all)[kind], chunk)

    def send(copy, chunk, before=None):
        def step(index):
            if before is not None:
                for earlier, place in before:
                    earlier(place, index).wait_send()
            copy(chunk, index).start()

        each_peer(step)

    arrange_loaded(0, 0)
    for load in lines[0][1]:
        load.start()
    for line in (0, token_rows + 1):
        for parity in range(2):
            shuffled[parity, line] = jnp.zeros(shuffled.shape[2:], jnp.bfloat16)
    pl.semaphore_wait(barrier, count - 1)
    send(copy_k, 0)
    for kinds in lines[1:]:
        for kind in kinds:
            for load in kind:
                load.start()
    for load in loads:
        load.start()
    arrange_loaded(0, 1)
    send(copy_q, 0)
    for chunk in range(1, chunks):
        arrange_loaded(chunk, 0)
        arrange_loaded(chunk, 1)

    for load in loads:
        load.wait()

    def within(window, carry):
        rows = attend_heads(
            qw[window],
            lambda start, stop: kw[window, :, start:stop],
            lambda start, stop: vw[window, :, start:stop],
            None,
        )
        for chunk in range(chunks):
            for place in range(pair):
                line = line_at(chunk, place)
                window_out[chunk, place, window] = rows[line * tile : (line + 1) * tile]
        return carry

    lax.fori_loop(0, windows, within, 0)

    def next_values(chunk, carry):
        arrange(window_out, v_mine, v_all, chunk)
        return carry

    lax.fori_loop(0, chunks, next_values, 0)
    send(copy_v, 0)

    def send_chunk(chunk):
        for copy in (copy_k, copy_q, copy_v):
            send(copy, chunk, [(copy, chunk - 1)])

    send_chunk(1)

    same = lax.rem(lax.broadcasted_iota(jnp.int32, square, 0), pair) == lax.rem(
        lax.broadcasted_iota(jnp.int32, square, 1), pair
    )

    def across(chunk):
        for copy in (copy_k, copy_q, copy_v):
            each_peer(lambda step: copy(chunk, step).wait_recv())
        mixed = attend_heads(
            flat(q_all)[chunk],
            lambda start, stop: flat(k_all)[chunk, :, start:stop],
            lambda start, stop: flat(v_all)[chunk, :, start:stop],
            same,
        )
        rows = jnp.dot(mixed, pw[...], preferred_element_type=jnp.float32) + pb[...]
        flat(proj)[chunk] = rows.astype(jnp.bfloat16)
        field[chunk, me] = proj[chunk, me]

    has_up, has_down = (my_row > 0, my_row < count_row - 1)
    first_col = my_col == 0

    shape = (pair * width, (count + 1) * block)
    row = lax.broadcasted_iota(jnp.int32, shape, 0)
    slot, place = (lax.rem(row, width), lax.div(row, width))
    token = jnp.where(slot <= wide, slot, slot - width)

    def source_row(column):
        inside = (column >= 0) & (column < wide)
        own = lax.rem(column + tile, tile) * block + lax.div(column + tile, tile) * pair - pair
        right = jnp.where((column == wide) & first_col, count * block, -token_rows)
        left = jnp.where(
            (column == -1) & (my_col > 0), count * block + (windows - 1) * pair, right
        )
        return jnp.where(inside, own, left) + place

    for shift in range(3):
        places[shift] = one_hot(source_row(token + shift - 1), shape)
    shape = (width, width)
    row = lax.broadcasted_iota(jnp.int32, shape, 0)
    for way in range(2):
        slides[way] = one_hot(lax.rem(row + width + 2 * way - 1, width), shape)

    def line_of(chunk, place):
        return chunk + 1 if place == 0 else token_rows - chunk

    near = jnp.where(first_col, count - 1, 0)
    turn = lax.rem(my_place - lax.rem(near, half) + half, half)
    first_step = jnp.where(
        near // half == my_half, half + lax.rem(turn - 1 + half, half), turn
    )

    def side(chunk):
        return pltpu.make_async_remote_copy(
            src_ref=field.at[chunk, near],
            dst_ref=field.at[chunk, count],
            send_sem=side_send.at[chunk],
            recv_sem=side_recv.at[chunk],
            device_id={"row": my_row, "col": 1 - my_col},
            device_id_type=pl.DeviceIdType.MESH,
        )

    def edge(parity, down):
        lanes = pl.ds(depth, 2 * depth)
        source, target = (token_rows, 0) if down else (1, token_rows + 1)
        place = 2 * parity + (1 if down else 0)
        return pltpu.make_async_remote_copy(
            src_ref=shuffled.at[parity, source, :, lanes],
            dst_ref=shuffled.at[parity, target, :, lanes],
            send_sem=edge_send.at[place],
            recv_sem=edge_recv.at[place],
            device_id={"row": my_row + (1 if down else -1), "col": my_col},
            device_id_type=pl.DeviceIdType.MESH,
        )

    seam = count_row // 2
    above, below = (my_row == seam - 1, my_row == seam)

    def relay(way):
        return pltpu.make_async_remote_copy(
            src_ref=seam_mine.at[way],
            dst_ref=seam_all.at[my_row, my_col],
            send_sem=seam_send.at[way],
            recv_sem=seam_recv.at[my_row],
            device_id={"row": jnp.where(way == 0, seam, seam - 1), "col": my_col},
            device_id_type=pl.DeviceIdType.MESH,
        )

    def seam_wait(owner):
        pltpu.make_async_remote_copy(
            src_ref=seam_mine.at[0],
            dst_ref=seam_all.at[owner, my_col],
            send_sem=seam_send.at[0],
            recv_sem=seam_recv.at[owner],
            device_id={"row": my_row, "col": 1 - my_col},
            device_id_type=pl.DeviceIdType.MESH,
        ).wait_recv()

    def seam_share():
        return pltpu.make_async_remote_copy(
            src_ref=seam_all.at[:, my_col],
            dst_ref=seam_all.at[:, my_col],
            send_sem=share_sem.at[0],
            recv_sem=share_sem.at[1],
            device_id={"row": my_row, "col": 1 - my_col},
            device_id_type=pl.DeviceIdType.MESH,
        )

    def send_seam():
        span = count_col * windows
        shape = (2 * span, count * block)
        row = lax.broadcasted_iota(jnp.int32, shape, 0)
        way, place = (lax.div(row, span), lax.rem(row, span))
        peer = (seam - 1 + way) * count_col + lax.div(place, windows)
        rows = one_hot(
            peer * block + lax.rem(place, windows) * pair + (1 - way) * (pair - 1), shape
        )
        rows = pick(rows, flat(proj)[0])
        for way, here in ((0, below), (1, above)):
            seam_mine[way] = rows[way * span : (way + 1) * span]

            @pl.when(here)
            def _():
                seam_all[my_row, my_col] = seam_mine[way]

            @pl.when(jnp.logical_not(here))
            def _():
                relay(way).start()

    def take_seam():
        def each(owner, carry):
            @pl.when(owner != my_row)
            def _():
                seam_wait(owner)

            return carry

        lax.fori_loop(0, count_row, each, 0)
        seam_share().start()
        seam_share().wait()

    def place_seam(line):
        span = count_col * windows
        source = seam_all.reshape(count * span, channels)
        shape = (width, count * span)
        row = lax.broadcasted_iota(jnp.int32, shape, 0)
        token = jnp.where(row <= wide, row, row - width)
        for shift in range(3):
            near_token = token + shift - 1
            column = near_token + my_col * wide
            known = (near_token >= -1) & (near_token <= wide)
            known = known & (column >= 0) & (column < count_col * wide)
            moved = column + tile
            target = lax.rem(moved, tile) * span + lax.div(moved, tile) - 1
            rows = one_hot(jnp.where(known, target, -1), shape)
            for parity in range(2):
                low = 2 * parity * depth
                start = (0, depth, 3 * depth)[shift]
                first = low + (depth if shift == 0 else 0)
                size = 2 * depth if shift == 1 else depth
                shuffled[parity, line, :, start : start + size] = pick(
                    rows, source[:, first : first + size]
                )

    sends_up, sends_down = (has_up & (my_row != seam), has_down & (my_row != seam - 1))
    edges = [(parity, down) for parity in range(2) for down in (True, False)]

    def build(chunk):
        copy_r(chunk, first_step).wait_recv()
        side(chunk).start()

        def rest(step):
            @pl.when(step != first_step)
            def _():
                copy_r(chunk, step).wait_recv()

        each_peer(rest)
        side(chunk).wait()
        source = field.reshape(chunks, (count + 1) * block, channels)
        for parity in range(2):
            low = 2 * parity * depth
            even, odd = (slice(low, low + depth), slice(low + depth, low + 2 * depth))
            both = slice(low, low + 2 * depth)
            for shift, lanes, start in ((0, odd, 0), (1, both, depth), (2, even, 3 * depth)):
                rows = pick(places[shift], source[chunk, :, lanes])
                stop = start + rows.shape[1]
                for place in range(pair):
                    shuffled[parity, line_of(chunk, place), :, start:stop] = rows[
                        place * width : (place + 1) * width
                    ]

    def finish_edges():
        for parity, down in edges:
            goes, comes = (sends_down, sends_up) if down else (sends_up, sends_down)

            @pl.when(goes)
            def _():
                edge(parity, down).wait_send()

            @pl.when(comes)
            def _():
                edge(parity, down).wait_recv()

        for here, line in ((below, 0), (above, token_rows + 1)):

            @pl.when(here)
            def _():
                take_seam()
                place_seam(line)

        for way, here in ((0, below), (1, above)):

            @pl.when(jnp.logical_not(here))
            def _():
                relay(way).wait_send()

        for parity in range(2):
            for line in (0, token_rows + 1):
                shuffled[parity, line, :, 0:depth] = pick(
                    slides[0], shuffled[parity, line, :, 2 * depth : 3 * depth]
                )
                shuffled[parity, line, :, 3 * depth :] = pick(
                    slides[1], shuffled[parity, line, :, depth : 2 * depth]
                )

    def convolve_lines(source, weights, parity, other, start, stop, columns):
        if parity == 0:
            taps = ((1, -1), (0, 0), (1, 0))
        else:
            taps = ((0, 0), (1, 0), (0, 1))
        cells = [
            source[
                plane, start + shift : stop + shift, 0:columns, other * depth : (other + 3) * depth
            ].reshape((stop - start) * columns, 3 * depth)
            for plane, shift in taps
        ]
        return jnp.dot(
            jnp.concatenate(cells, axis=1),
            weights.reshape(weights.shape[0] * weights.shape[1], depth)[...],
            preferred_element_type=jnp.float32,
        )

    edge_slot = lax.broadcasted_iota(jnp.int32, (width - wide, depth), 0)
    valid = edge_slot == jnp.where(first_col, 0, width - wide - 1)

    def activate(parity, start, stop):
        for other in range(2):
            value = convolve_lines(shuffled, fk, parity, other, start, stop, width)
            value = jax.nn.gelu(value + fb[...])
            for line in range(start, stop):
                cells = value[(line - start) * width : (line - start + 1) * width]
                cells = jnp.concatenate(
                    [cells[:wide], jnp.where(valid, cells[wide:], 0.0)], axis=0
                )
                if line == 0:
                    cells = jnp.where(has_up, cells, 0.0)
                if line == token_rows + 1:
                    cells = jnp.where(has_down, cells, 0.0)
                activated[parity, line, :, (other + 1) * depth : (other + 2) * depth] = (
                    cells.astype(jnp.bfloat16)
                )
                if other == 1:
                    moved = pltpu.roll(cells, 1, 0)
                    activated[parity, line, :, 0:depth] = moved.astype(jnp.bfloat16)
                else:
                    moved = pltpu.roll(cells, width - 1, 0)
                    activated[parity, line, :, 3 * depth :] = moved.astype(jnp.bfloat16)

    def emit(start, stop):
        for parity in range(2):
            for other in range(2):
                value = convolve_lines(activated, sk, parity, other, start, stop, wide)
                value = value + sb[...]
                for line in range(start, stop):
                    rows = slice((line - start) * wide, (line - start + 1) * wide)
                    for part in range(depth // LANES):
                        stage[2 * line - 2 + parity, part, pl.ds(other, wide, stride=2), :] = (
                            value[rows, part * LANES : (part + 1) * LANES]
                        )
            for line in range(start, stop):
                place = 2 * line - 2 + parity
                for part in range(depth // LANES):
                    lanes = slice(part * LANES, (part + 1) * LANES)
                    out[place, :, lanes] = stage[place, part].astype(jnp.bfloat16)

    def finish(chunk):
        build(chunk)
        top, low = (chunk + 1, token_rows - chunk)
        if chunk == 0:
            for parity, down in edges:

                @pl.when(sends_down if down else sends_up)
                def _():
                    edge(parity, down).start()

            return
        if chunk == 1:
            finish_edges()
            activate(1, 0, 1)
            activate(0, token_rows + 1, token_rows + 2)
            activate(0, 1, 2)
            activate(1, token_rows, token_rows + 1)
        if chunk < chunks - 1:
            activate(1, top - 1, top)
            activate(0, top, top + 1)
            activate(0, low + 1, low + 2)
            activate(1, low, low + 1)
            spans = ((top - 1, top), (low + 1, low + 2))
        else:
            activate(1, top - 1, low + 1)
            activate(0, top, low + 2)
            spans = ((top - 1, low + 2),)
        for span in spans:
            emit(*span)

    last = chunks - 1
    for chunk in range(chunks):
        across(chunk)
        if chunk < last - 1:
            send(copy_r, chunk)
            if chunk == 0:
                send_seam()
            send_chunk(chunk + 2)
            if chunk > 0:
                finish(chunk - 1)
        elif chunk < last:
            finish(chunk - 1)
            send(copy_r, chunk, [(copy, last) for copy in (copy_k, copy_q, copy_v)])
        else:
            send(copy_r, chunk, [(copy_r, chunk - 1)])
    finish(last - 1)
    finish(last)
    for chunk in (*range(last - 1), last):
        each_peer(lambda step: copy_r(chunk, step).wait_send())


def fused(qw, kw, vw, qi, ki, proj_weight, proj_bias, first_kernel, first_bias, second_kernel, second_bias):
    windows, tokens_win, features = qw.shape
    count_row = lax.axis_size("row")
    count_col = lax.axis_size("col")
    count = count_row * count_col
    channels = proj_weight.shape[-1]
    depth = first_kernel.shape[-1]
    taps = (first_kernel.shape[0], first_kernel.shape[1] * first_kernel.shape[2], depth)
    token_rows = tokens_win // TILE_COLS
    chunks = token_rows // LINES
    block = windows * LINES
    width = (windows + 1) * TILE_COLS
    planes = (2, token_rows + 2, width, 4 * depth)
    fine = (2 * token_rows, 2 * windows * TILE_COLS, depth)
    rows = (chunks, count, block, features)
    lines = (chunks, LINES, windows, TILE_COLS, features)
    whole = pl.BlockSpec(memory_space=pl.ANY)
    held = pl.BlockSpec(memory_space=pltpu.VMEM)
    dma = pltpu.SemaphoreType.DMA
    return pl.pallas_call(
        functools.partial(attention_kernel, count_row, count_col),
        out_shape=pltpu.VMEM(fine, jnp.bfloat16),
        in_specs=[whole] * 11,
        out_specs=held,
        scratch_shapes=[pltpu.VMEM(qw.shape, jnp.bfloat16)] * 3
        + [pltpu.VMEM(lines, jnp.bfloat16)] * 2
        + [
            pltpu.VMEM(proj_weight.shape, jnp.bfloat16),
            pltpu.VMEM(taps, jnp.bfloat16),
            pltpu.VMEM(taps, jnp.bfloat16),
            pltpu.VMEM((1, channels), jnp.float32),
            pltpu.VMEM((1, depth), jnp.float32),
            pltpu.VMEM((1, depth), jnp.float32),
            pltpu.VMEM(lines, jnp.bfloat16),
            pltpu.VMEM((count * block, count * block), jnp.bfloat16),
        ]
        + [pltpu.VMEM(rows, jnp.bfloat16)] * 6
        + [
            pltpu.VMEM((chunks, count, block, channels), jnp.bfloat16),
            pltpu.VMEM((chunks, count + 1, block, channels), jnp.bfloat16),
            pltpu.VMEM((2, count_col * windows, channels), jnp.bfloat16),
            pltpu.VMEM((count_row, count_col, count_col * windows, channels), jnp.bfloat16),
            pltpu.VMEM((3, LINES * width, (count + 1) * block), jnp.bfloat16),
            pltpu.VMEM((2, width, width), jnp.bfloat16),
            pltpu.VMEM(planes, jnp.bfloat16),
            pltpu.VMEM(planes, jnp.bfloat16),
            pltpu.VMEM((fine[0], depth // LANES, fine[1], LANES), jnp.float32),
            dma((9,)),
            dma((chunks, LINES)),
            dma((chunks, LINES)),
        ]
        + [dma((chunks, count))] * 8
        + [
            dma((chunks,)),
            dma((chunks,)),
            dma((4,)),
            dma((4,)),
            dma((2,)),
            dma((count_row,)),
            dma((2,)),
        ],
        compiler_params=pltpu.CompilerParams(
            collective_id=0, has_side_effects=True, vmem_limit_bytes=60 * 1024 * 1024
        ),
    )(
        qw,
        kw,
        vw,
        qi,
        ki,
        proj_weight,
        first_kernel.reshape(taps),
        second_kernel.reshape(taps),
        proj_bias.reshape(1, channels),
        first_bias.reshape(1, depth),
        second_bias.reshape(1, depth),
    )


def convolutions(
    projected, rows_dev, cols_dev, first_kernel, first_bias, second_kernel, second_bias
):
    grouped = projected.reshape(rows_dev, cols_dev, TILE_ROWS, TILE_COLS, 2, 2, CHANNELS)
    shuffled = jnp.transpose(grouped, (0, 2, 4, 1, 3, 5, 6)).reshape(
        rows_dev * TILE_ROWS * 2, cols_dev * TILE_COLS * 2, CHANNELS
    )
    activated = jax.nn.gelu(convolve(shuffled, first_kernel, first_bias)).astype(jnp.bfloat16)
    return convolve(activated, second_kernel, second_bias).astype(jnp.bfloat16)


def shards(
    query_window,
    key_window,
    value_window,
    query_index,
    key_index,
    proj_weight,
    proj_bias,
    first_kernel,
    first_bias,
    second_kernel,
    second_bias,
):
    rows_dev, cols_dev, tokens_win, features = query_window.shape
    flat = (rows_dev * cols_dev, tokens_win, features)
    owners = lax.axis_size("row") * lax.axis_size("col")
    fits = rows_dev == 1 and lax.axis_size("col") == 2 and owners == TILE_COLS
    fits = fits and tokens_win % (LINES * TILE_COLS) == 0 and tokens_win >= 4 * LINES * TILE_COLS
    if fits and cols_dev * LINES % 8 == 0 and features % LANES == 0:
        return fused(
            query_window.reshape(flat),
            key_window.reshape(flat),
            value_window.reshape(flat),
            query_index.reshape(flat),
            key_index.reshape(flat),
            proj_weight,
            proj_bias,
            first_kernel,
            first_bias,
            second_kernel,
            second_bias,
        )
    layout = (rows_dev * cols_dev, tokens_win, HEADS, HEAD_DIM)
    window_out = window_attend(
        query_window.reshape(layout), key_window.reshape(layout), value_window.reshape(layout)
    ).reshape(query_window.shape)
    count_row = lax.axis_size("row")
    count_col = lax.axis_size("col")
    owned_tokens = tokens_win // (count_row * count_col)
    moved = (
        lax.all_to_all(query_index, ("row", "col"), split_axis=2, concat_axis=0, tiled=True),
        lax.all_to_all(key_index, ("row", "col"), split_axis=2, concat_axis=0, tiled=True),
        lax.all_to_all(window_out, ("row", "col"), split_axis=2, concat_axis=0, tiled=True),
    )
    owner_shape = moved[0].shape
    across = (-1, owned_tokens, HEADS, HEAD_DIM)
    index_out = index_attend(
        moved[0].reshape(across), moved[1].reshape(across), moved[2].reshape(across)
    )
    index_rows = index_out.reshape(-1, features)
    owner_rows = (
        jnp.dot(index_rows, proj_weight, preferred_element_type=jnp.float32) + proj_bias
    ).astype(jnp.bfloat16)
    last = owner_rows.shape[-1]
    shaped = owner_rows.reshape(tuple(owner_shape[:-1]) + (last,))
    returned = lax.all_to_all(shaped, ("row", "col"), split_axis=0, concat_axis=2, tiled=True)
    projected = returned.reshape(rows_dev * cols_dev * tokens_win, last)
    return convolutions(
        projected, rows_dev, cols_dev, first_kernel, first_bias, second_kernel, second_bias
    )


def solution(mesh):
    in_specs = (
        P(("grp", "row"), "col", None, None),
        P(("grp", "row"), "col", None, None),
        P(("grp", "row"), "col", None, None),
        P(("grp", "row"), "col", None, None),
        P(("grp", "row"), "col", None, None),
        P(),
        P(),
        P(),
        P(),
        P(),
        P(),
    )
    out_specs = P(("grp", "row"), "col", None)
    return jax.shard_map(shards, mesh=mesh, in_specs=in_specs, out_specs=out_specs, check_vma=False)
```

```python
import functools
import math

import jax
import jax.numpy as jnp
from jax import lax
from jax.experimental import pallas as pl
from jax.experimental.pallas import tpu as pltpu
from jax.sharding import PartitionSpec as P

HEADS = 8
HEAD_DIM = 160
CHANNELS = 256
TILE_ROWS = 8
TILE_COLS = 16
LANES = 128
LINES = 2


def extended(value, sides, width):
    for axis, dim in sides:
        size, length = (lax.axis_size(axis), value.shape[dim])
        up = [(i, (i + 1) % size) for i in range(size - 1)]
        down = [(j, i) for i, j in up]
        last = lax.slice_in_dim(value, length - width, length, axis=dim)
        first = lax.slice_in_dim(value, 0, width, axis=dim)
        before = lax.ppermute(last, axis, up)
        after = lax.ppermute(first, axis, down)
        value = jnp.concatenate([before, value, after], axis=dim)
    return value


def softmax_rows(scores):
    highest = jnp.max(scores, axis=-1, keepdims=True)
    raised = jnp.exp(scores - highest)
    return (raised / jnp.sum(raised, axis=-1, keepdims=True)).astype(jnp.bfloat16)


def window_attend(queries, key_rows, values):
    scores = jnp.einsum(
        "blhd,bmhd->bhlm", queries, key_rows, preferred_element_type=jnp.float32
    ) / math.sqrt(HEAD_DIM)
    weights = softmax_rows(scores)
    return jnp.einsum(
        "bhlm,bmhd->blhd", weights, values, preferred_element_type=jnp.float32
    ).astype(jnp.bfloat16)


def index_attend(queries, key_rows, values):
    scores = jnp.einsum(
        "lbhd,mbhd->bhlm", queries, key_rows, preferred_element_type=jnp.float32
    ) / math.sqrt(HEAD_DIM)
    weights = softmax_rows(scores)
    return jnp.einsum(
        "bhlm,mbhd->lbhd", weights, values, preferred_element_type=jnp.float32
    ).astype(jnp.bfloat16)


def convolve(image, kernel, bias):
    height, breadth, depth = image.shape
    padded = extended(image, (("row", 0), ("col", 1)), 1)
    total = jnp.zeros((height * breadth, kernel.shape[-1]), jnp.float32)
    for row_shift in range(3):
        for col_shift in range(3):
            cells = padded[row_shift : row_shift + height, col_shift : col_shift + breadth].reshape(
                -1, depth
            )
            total = total + jnp.dot(
                cells, kernel[row_shift, col_shift], preferred_element_type=jnp.float32
            )
    return (total + bias).reshape(height, breadth, -1)


def attend_heads(queries, key_part, value_part, same):
    rows, features = queries.shape
    head_dim = features // HEADS
    factor = math.log2(math.e) / math.sqrt(head_dim)
    blocks = [None] * (features // LANES)
    for head in range(HEADS):
        low, high = (head * head_dim, (head + 1) * head_dim)
        start, stop = (low // LANES * LANES, -(-high // LANES) * LANES)
        lane = lax.broadcasted_iota(jnp.int32, (rows, stop - start), 1) + start
        inside = (lane >= low) & (lane < high)
        part = queries[:, start:stop]
        part = jnp.where(inside, part, jnp.zeros_like(part))
        scores = lax.dot_general(
            part,
            key_part(start, stop),
            (((1,), (1,)), ((), ())),
            preferred_element_type=jnp.float32,
        )
        if same is not None:
            scores = jnp.where(same, scores, -1e30)
        highest = jnp.max(scores, axis=-1, keepdims=True)
        raised = jnp.exp2((scores - highest) * factor)
        weights = (raised * (1.0 / jnp.sum(raised, axis=-1, keepdims=True))).astype(jnp.bfloat16)
        mixed = jnp.dot(weights, value_part(start, stop), preferred_element_type=jnp.float32)
        mixed = jnp.where(inside, mixed, 0.0)
        for block in range(start // LANES, stop // LANES):
            piece = mixed[:, block * LANES - start : (block + 1) * LANES - start]
            blocks[block] = piece if blocks[block] is None else blocks[block] + piece
    return jnp.concatenate(blocks, axis=1).astype(jnp.bfloat16)


def one_hot(target, shape):
    return (lax.broadcasted_iota(jnp.int32, shape, 1) == target).astype(jnp.bfloat16)


def pick(rows, source):
    return jnp.dot(rows, source, preferred_element_type=jnp.float32).astype(jnp.bfloat16)


def attention_kernel(
    count_row,
    count_col,
    qw_hbm,
    kw_hbm,
    vw_hbm,
    qi_hbm,
    ki_hbm,
    pw_hbm,
    fk_hbm,
    sk_hbm,
    pb_hbm,
    fb_hbm,
    sb_hbm,
    out,
    qw,
    kw,
    vw,
    qi,
    ki,
    pw,
    fk,
    sk,
    pb,
    fb,
    sb,
    window_out,
    order,
    k_mine,
    q_mine,
    v_mine,
    k_all,
    q_all,
    v_all,
    proj,
    field,
    seam_mine,
    seam_all,
    places,
    slides,
    shuffled,
    activated,
    stage,
    load_sem,
    ki_sem,
    qi_sem,
    k_send,
    k_recv,
    q_send,
    q_recv,
    v_send,
    v_recv,
    r_send,
    r_recv,
    side_send,
    side_recv,
    edge_send,
    edge_recv,
    seam_send,
    seam_recv,
    share_sem,
):
    count = count_row * count_col
    half = count // 2
    windows, tokens_win, features = qw.shape
    tile = TILE_COLS
    token_rows = tokens_win // tile
    chunks, _, block, channels = proj.shape
    pair = block // windows
    wide = windows * tile
    width = shuffled.shape[2]
    depth = fk.shape[-1]
    my_row, my_col = (lax.axis_index("row"), lax.axis_index("col"))
    me = my_row * count_col + my_col
    my_half, my_place = (me // half, lax.rem(me, half))

    def peer_of(step):
        across = (1 - my_half) * half + lax.rem(my_place + step, half)
        beside = my_half * half + lax.rem(my_place + step + 1, half)
        return jnp.where(step < half, across, beside)

    def device(peer):
        return {"row": peer // count_col, "col": lax.rem(peer, count_col)}

    def each_peer(body):
        def step(index, carry):
            body(index)
            return carry

        lax.fori_loop(0, count - 1, step, 0, unroll=5)

    def line_at(chunk, place):
        return chunk if place == 0 else token_rows - 1 - chunk

    def load_lines(source, target, sems, chunk):
        return [
            pltpu.make_async_copy(
                source.at[:, pl.ds(line_at(chunk, place) * tile, tile), :],
                target.at[chunk, place],
                sems.at[chunk, place],
            )
            for place in range(pair)
        ]

    pairs = ((ki_hbm, ki, ki_sem), (qi_hbm, qi, qi_sem))
    lines = [[load_lines(*kind, chunk) for kind in pairs] for chunk in range(chunks)]
    loads = [
        pltpu.make_async_copy(source, target, load_sem.at[place])
        for place, (source, target) in enumerate(
            (
                (qw_hbm, qw),
                (kw_hbm, kw),
                (vw_hbm, vw),
                (pw_hbm, pw),
                (fk_hbm, fk),
                (sk_hbm, sk),
                (pb_hbm, pb),
                (fb_hbm, fb),
                (sb_hbm, sb),
            )
        )
    ]
    for load in lines[0][0]:
        load.start()

    barrier = pltpu.get_barrier_semaphore()

    def greet(step):
        pl.semaphore_signal(
            barrier,
            inc=1,
            device_id=device(peer_of(step)),
            device_id_type=pl.DeviceIdType.MESH,
        )

    each_peer(greet)

    def sender(source, target, sems):
        def copy(chunk, step):
            peer = peer_of(step)
            return pltpu.make_async_remote_copy(
                src_ref=source.at[chunk, peer],
                dst_ref=target.at[chunk, me],
                send_sem=sems[0].at[chunk, step],
                recv_sem=sems[1].at[chunk, step],
                device_id=device(peer),
                device_id_type=pl.DeviceIdType.MESH,
            )

        return copy

    copy_k = sender(k_mine, k_all, (k_send, k_recv))
    copy_q = sender(q_mine, q_all, (q_send, q_recv))
    copy_v = sender(v_mine, v_all, (v_send, v_recv))
    copy_r = sender(proj, field, (r_send, r_recv))

    def flat(ref):
        return ref.reshape(chunks, count * block, ref.shape[-1])

    square = (count * block, count * block)
    row = lax.broadcasted_iota(jnp.int32, square, 0)
    order[...] = one_hot(
        lax.rem(row, pair) * wide + lax.div(lax.rem(row, block), pair) * tile + lax.div(row, block),
        square,
    )

    def arrange(source, mine, everyone, chunk):
        rows = source.reshape(chunks, count * block, features)[chunk]
        flat(mine)[chunk] = pick(order[...], rows)
        everyone[chunk, me] = mine[chunk, me]

    def arrange_loaded(chunk, kind):
        for load in lines[chunk][kind]:
            load.wait()
        arrange((ki, qi)[kind], (k_mine, q_mine)[kind], (k_all, q_all)[kind], chunk)

    def send(copy, chunk, before=None):
        def step(index):
            if before is not None:
                for earlier, place in before:
                    earlier(place, index).wait_send()
            copy(chunk, index).start()

        each_peer(step)

    arrange_loaded(0, 0)
    for load in lines[0][1]:
        load.start()
    for line in (0, token_rows + 1):
        for parity in range(2):
            shuffled[parity, line] = jnp.zeros(shuffled.shape[2:], jnp.bfloat16)
    pl.semaphore_wait(barrier, count - 1)
    send(copy_k, 0)
    for kinds in lines[1:]:
        for kind in kinds:
            for load in kind:
                load.start()
    for load in loads:
        load.start()
    arrange_loaded(0, 1)
    send(copy_q, 0)
    for chunk in range(1, chunks):
        arrange_loaded(chunk, 0)
        arrange_loaded(chunk, 1)

    for load in loads:
        load.wait()

    def within(window, carry):
        rows = attend_heads(
            qw[window],
            lambda start, stop: kw[window, :, start:stop],
            lambda start, stop: vw[window, :, start:stop],
            None,
        )
        for chunk in range(chunks):
            for place in range(pair):
                line = line_at(chunk, place)
                window_out[chunk, place, window] = rows[line * tile : (line + 1) * tile]
        return carry

    lax.fori_loop(0, windows, within, 0)

    def next_values(chunk, carry):
        arrange(window_out, v_mine, v_all, chunk)
        return carry

    lax.fori_loop(0, chunks, next_values, 0)
    send(copy_v, 0)

    def send_chunk(chunk):
        for copy in (copy_k, copy_q, copy_v):
            send(copy, chunk, [(copy, chunk - 1)])

    send_chunk(1)

    same = lax.rem(lax.broadcasted_iota(jnp.int32, square, 0), pair) == lax.rem(
        lax.broadcasted_iota(jnp.int32, square, 1), pair
    )

    def across(chunk):
        for copy in (copy_k, copy_q, copy_v):
            each_peer(lambda step: copy(chunk, step).wait_recv())
        mixed = attend_heads(
            flat(q_all)[chunk],
            lambda start, stop: flat(k_all)[chunk, :, start:stop],
            lambda start, stop: flat(v_all)[chunk, :, start:stop],
            same,
        )
        rows = jnp.dot(mixed, pw[...], preferred_element_type=jnp.float32) + pb[...]
        flat(proj)[chunk] = rows.astype(jnp.bfloat16)
        field[chunk, me] = proj[chunk, me]

    has_up, has_down = (my_row > 0, my_row < count_row - 1)
    first_col = my_col == 0

    shape = (pair * width, (count + 1) * block)
    row = lax.broadcasted_iota(jnp.int32, shape, 0)
    slot, place = (lax.rem(row, width), lax.div(row, width))
    token = jnp.where(slot <= wide, slot, slot - width)

    def source_row(column):
        inside = (column >= 0) & (column < wide)
        own = lax.rem(column + tile, tile) * block + lax.div(column + tile, tile) * pair - pair
        right = jnp.where((column == wide) & first_col, count * block, -token_rows)
        left = jnp.where(
            (column == -1) & (my_col > 0), count * block + (windows - 1) * pair, right
        )
        return jnp.where(inside, own, left) + place

    for shift in range(3):
        places[shift] = one_hot(source_row(token + shift - 1), shape)
    shape = (width, width)
    row = lax.broadcasted_iota(jnp.int32, shape, 0)
    for way in range(2):
        slides[way] = one_hot(lax.rem(row + width + 2 * way - 1, width), shape)

    def line_of(chunk, place):
        return chunk + 1 if place == 0 else token_rows - chunk

    near = jnp.where(first_col, count - 1, 0)
    turn = lax.rem(my_place - lax.rem(near, half) + half, half)
    first_step = jnp.where(
        near // half == my_half, half + lax.rem(turn - 1 + half, half), turn
    )

    def side(chunk):
        return pltpu.make_async_remote_copy(
            src_ref=field.at[chunk, near],
            dst_ref=field.at[chunk, count],
            send_sem=side_send.at[chunk],
            recv_sem=side_recv.at[chunk],
            device_id={"row": my_row, "col": 1 - my_col},
            device_id_type=pl.DeviceIdType.MESH,
        )

    def edge(parity, down):
        lanes = pl.ds(depth, 2 * depth)
        source, target = (token_rows, 0) if down else (1, token_rows + 1)
        place = 2 * parity + (1 if down else 0)
        return pltpu.make_async_remote_copy(
            src_ref=shuffled.at[parity, source, :, lanes],
            dst_ref=shuffled.at[parity, target, :, lanes],
            send_sem=edge_send.at[place],
            recv_sem=edge_recv.at[place],
            device_id={"row": my_row + (1 if down else -1), "col": my_col},
            device_id_type=pl.DeviceIdType.MESH,
        )

    seam = count_row // 2
    above, below = (my_row == seam - 1, my_row == seam)

    def relay(way):
        return pltpu.make_async_remote_copy(
            src_ref=seam_mine.at[way],
            dst_ref=seam_all.at[my_row, my_col],
            send_sem=seam_send.at[way],
            recv_sem=seam_recv.at[my_row],
            device_id={"row": jnp.where(way == 0, seam, seam - 1), "col": my_col},
            device_id_type=pl.DeviceIdType.MESH,
        )

    def seam_wait(owner):
        pltpu.make_async_remote_copy(
            src_ref=seam_mine.at[0],
            dst_ref=seam_all.at[owner, my_col],
            send_sem=seam_send.at[0],
            recv_sem=seam_recv.at[owner],
            device_id={"row": my_row, "col": 1 - my_col},
            device_id_type=pl.DeviceIdType.MESH,
        ).wait_recv()

    def seam_share():
        return pltpu.make_async_remote_copy(
            src_ref=seam_all.at[:, my_col],
            dst_ref=seam_all.at[:, my_col],
            send_sem=share_sem.at[0],
            recv_sem=share_sem.at[1],
            device_id={"row": my_row, "col": 1 - my_col},
            device_id_type=pl.DeviceIdType.MESH,
        )

    def send_seam():
        span = count_col * windows
        shape = (2 * span, count * block)
        row = lax.broadcasted_iota(jnp.int32, shape, 0)
        way, place = (lax.div(row, span), lax.rem(row, span))
        peer = (seam - 1 + way) * count_col + lax.div(place, windows)
        rows = one_hot(
            peer * block + lax.rem(place, windows) * pair + (1 - way) * (pair - 1), shape
        )
        rows = pick(rows, flat(proj)[0])
        for way, here in ((0, below), (1, above)):
            seam_mine[way] = rows[way * span : (way + 1) * span]

            @pl.when(here)
            def _():
                seam_all[my_row, my_col] = seam_mine[way]

            @pl.when(jnp.logical_not(here))
            def _():
                relay(way).start()

    def take_seam():
        def each(owner, carry):
            @pl.when(owner != my_row)
            def _():
                seam_wait(owner)

            return carry

        lax.fori_loop(0, count_row, each, 0)
        seam_share().start()
        seam_share().wait()

    def place_seam(line):
        span = count_col * windows
        source = seam_all.reshape(count * span, channels)
        shape = (width, count * span)
        row = lax.broadcasted_iota(jnp.int32, shape, 0)
        token = jnp.where(row <= wide, row, row - width)
        for shift in range(3):
            near_token = token + shift - 1
            column = near_token + my_col * wide
            known = (near_token >= -1) & (near_token <= wide)
            known = known & (column >= 0) & (column < count_col * wide)
            moved = column + tile
            target = lax.rem(moved, tile) * span + lax.div(moved, tile) - 1
            rows = one_hot(jnp.where(known, target, -1), shape)
            for parity in range(2):
                low = 2 * parity * depth
                start = (0, depth, 3 * depth)[shift]
                first = low + (depth if shift == 0 else 0)
                size = 2 * depth if shift == 1 else depth
                shuffled[parity, line, :, start : start + size] = pick(
                    rows, source[:, first : first + size]
                )

    sends_up, sends_down = (has_up & (my_row != seam), has_down & (my_row != seam - 1))
    edges = [(parity, down) for parity in range(2) for down in (True, False)]

    def build(chunk):
        copy_r(chunk, first_step).wait_recv()
        side(chunk).start()

        def rest(step):
            @pl.when(step != first_step)
            def _():
                copy_r(chunk, step).wait_recv()

        each_peer(rest)
        side(chunk).wait()
        source = field.reshape(chunks, (count + 1) * block, channels)
        for parity in range(2):
            low = 2 * parity * depth
            even, odd = (slice(low, low + depth), slice(low + depth, low + 2 * depth))
            both = slice(low, low + 2 * depth)
            for shift, lanes, start in ((0, odd, 0), (1, both, depth), (2, even, 3 * depth)):
                rows = pick(places[shift], source[chunk, :, lanes])
                stop = start + rows.shape[1]
                for place in range(pair):
                    shuffled[parity, line_of(chunk, place), :, start:stop] = rows[
                        place * width : (place + 1) * width
                    ]

    def finish_edges():
        for parity, down in edges:
            goes, comes = (sends_down, sends_up) if down else (sends_up, sends_down)

            @pl.when(goes)
            def _():
                edge(parity, down).wait_send()

            @pl.when(comes)
            def _():
                edge(parity, down).wait_recv()

        for here, line in ((below, 0), (above, token_rows + 1)):

            @pl.when(here)
            def _():
                take_seam()
                place_seam(line)

        for way, here in ((0, below), (1, above)):

            @pl.when(jnp.logical_not(here))
            def _():
                relay(way).wait_send()

        for parity in range(2):
            for line in (0, token_rows + 1):
                shuffled[parity, line, :, 0:depth] = pick(
                    slides[0], shuffled[parity, line, :, 2 * depth : 3 * depth]
                )
                shuffled[parity, line, :, 3 * depth :] = pick(
                    slides[1], shuffled[parity, line, :, depth : 2 * depth]
                )

    def convolve_lines(source, weights, parity, other, start, stop, columns):
        if parity == 0:
            taps = ((1, -1), (0, 0), (1, 0))
        else:
            taps = ((0, 0), (1, 0), (0, 1))
        cells = [
            source[
                plane, start + shift : stop + shift, 0:columns, other * depth : (other + 3) * depth
            ].reshape((stop - start) * columns, 3 * depth)
            for plane, shift in taps
        ]
        return jnp.dot(
            jnp.concatenate(cells, axis=1),
            weights.reshape(weights.shape[0] * weights.shape[1], depth)[...],
            preferred_element_type=jnp.float32,
        )

    edge_slot = lax.broadcasted_iota(jnp.int32, (width - wide, depth), 0)
    valid = edge_slot == jnp.where(first_col, 0, width - wide - 1)

    def activate(parity, start, stop):
        for other in range(2):
            value = convolve_lines(shuffled, fk, parity, other, start, stop, width)
            value = jax.nn.gelu(value + fb[...])
            for line in range(start, stop):
                cells = value[(line - start) * width : (line - start + 1) * width]
                cells = jnp.concatenate(
                    [cells[:wide], jnp.where(valid, cells[wide:], 0.0)], axis=0
                )
                if line == 0:
                    cells = jnp.where(has_up, cells, 0.0)
                if line == token_rows + 1:
                    cells = jnp.where(has_down, cells, 0.0)
                activated[parity, line, :, (other + 1) * depth : (other + 2) * depth] = (
                    cells.astype(jnp.bfloat16)
                )
                if other == 1:
                    moved = pltpu.roll(cells, 1, 0)
                    activated[parity, line, :, 0:depth] = moved.astype(jnp.bfloat16)
                else:
                    moved = pltpu.roll(cells, width - 1, 0)
                    activated[parity, line, :, 3 * depth :] = moved.astype(jnp.bfloat16)

    def emit(start, stop):
        for parity in range(2):
            for other in range(2):
                value = convolve_lines(activated, sk, parity, other, start, stop, wide)
                value = value + sb[...]
                for line in range(start, stop):
                    rows = slice((line - start) * wide, (line - start + 1) * wide)
                    for part in range(depth // LANES):
                        stage[2 * line - 2 + parity, part, pl.ds(other, wide, stride=2), :] = (
                            value[rows, part * LANES : (part + 1) * LANES]
                        )
            for line in range(start, stop):
                place = 2 * line - 2 + parity
                for part in range(depth // LANES):
                    lanes = slice(part * LANES, (part + 1) * LANES)
                    out[place, :, lanes] = stage[place, part].astype(jnp.bfloat16)

    def finish(chunk):
        build(chunk)
        top, low = (chunk + 1, token_rows - chunk)
        if chunk == 0:
            for parity, down in edges:

                @pl.when(sends_down if down else sends_up)
                def _():
                    edge(parity, down).start()

            return
        if chunk == 1:
            finish_edges()
            activate(1, 0, 1)
            activate(0, token_rows + 1, token_rows + 2)
            activate(0, 1, 2)
            activate(1, token_rows, token_rows + 1)
        if chunk < chunks - 1:
            activate(1, top - 1, top)
            activate(0, top, top + 1)
            activate(0, low + 1, low + 2)
            activate(1, low, low + 1)
            spans = ((top - 1, top), (low + 1, low + 2))
        else:
            activate(1, top - 1, low + 1)
            activate(0, top, low + 2)
            spans = ((top - 1, low + 2),)
        for span in spans:
            emit(*span)

    last = chunks - 1
    for chunk in range(chunks):
        across(chunk)
        if chunk < last - 1:
            send(copy_r, chunk)
            if chunk == 0:
                send_seam()
            send_chunk(chunk + 2)
            if chunk > 0:
                finish(chunk - 1)
        elif chunk < last:
            finish(chunk - 1)
            send(copy_r, chunk, [(copy, last) for copy in (copy_k, copy_q, copy_v)])
        else:
            send(copy_r, chunk)
    finish(last - 1)
    finish(last)
    for chunk in range(chunks):
        each_peer(lambda step: copy_r(chunk, step).wait_send())


def fused(qw, kw, vw, qi, ki, proj_weight, proj_bias, first_kernel, first_bias, second_kernel, second_bias):
    windows, tokens_win, features = qw.shape
    count_row = lax.axis_size("row")
    count_col = lax.axis_size("col")
    count = count_row * count_col
    channels = proj_weight.shape[-1]
    depth = first_kernel.shape[-1]
    taps = (first_kernel.shape[0], first_kernel.shape[1] * first_kernel.shape[2], depth)
    token_rows = tokens_win // TILE_COLS
    chunks = token_rows // LINES
    block = windows * LINES
    width = (windows + 1) * TILE_COLS
    planes = (2, token_rows + 2, width, 4 * depth)
    fine = (2 * token_rows, 2 * windows * TILE_COLS, depth)
    rows = (chunks, count, block, features)
    lines = (chunks, LINES, windows, TILE_COLS, features)
    whole = pl.BlockSpec(memory_space=pl.ANY)
    held = pl.BlockSpec(memory_space=pltpu.VMEM)
    dma = pltpu.SemaphoreType.DMA
    return pl.pallas_call(
        functools.partial(attention_kernel, count_row, count_col),
        out_shape=pltpu.VMEM(fine, jnp.bfloat16),
        in_specs=[whole] * 11,
        out_specs=held,
        scratch_shapes=[pltpu.VMEM(qw.shape, jnp.bfloat16)] * 3
        + [pltpu.VMEM(lines, jnp.bfloat16)] * 2
        + [
            pltpu.VMEM(proj_weight.shape, jnp.bfloat16),
            pltpu.VMEM(taps, jnp.bfloat16),
            pltpu.VMEM(taps, jnp.bfloat16),
            pltpu.VMEM((1, channels), jnp.float32),
            pltpu.VMEM((1, depth), jnp.float32),
            pltpu.VMEM((1, depth), jnp.float32),
            pltpu.VMEM(lines, jnp.bfloat16),
            pltpu.VMEM((count * block, count * block), jnp.bfloat16),
        ]
        + [pltpu.VMEM(rows, jnp.bfloat16)] * 6
        + [
            pltpu.VMEM((chunks, count, block, channels), jnp.bfloat16),
            pltpu.VMEM((chunks, count + 1, block, channels), jnp.bfloat16),
            pltpu.VMEM((2, count_col * windows, channels), jnp.bfloat16),
            pltpu.VMEM((count_row, count_col, count_col * windows, channels), jnp.bfloat16),
            pltpu.VMEM((3, LINES * width, (count + 1) * block), jnp.bfloat16),
            pltpu.VMEM((2, width, width), jnp.bfloat16),
            pltpu.VMEM(planes, jnp.bfloat16),
            pltpu.VMEM(planes, jnp.bfloat16),
            pltpu.VMEM((fine[0], depth // LANES, fine[1], LANES), jnp.float32),
            dma((9,)),
            dma((chunks, LINES)),
            dma((chunks, LINES)),
        ]
        + [dma((chunks, count))] * 8
        + [
            dma((chunks,)),
            dma((chunks,)),
            dma((4,)),
            dma((4,)),
            dma((2,)),
            dma((count_row,)),
            dma((2,)),
        ],
        compiler_params=pltpu.CompilerParams(
            collective_id=0, has_side_effects=True, vmem_limit_bytes=60 * 1024 * 1024
        ),
    )(
        qw,
        kw,
        vw,
        qi,
        ki,
        proj_weight,
        first_kernel.reshape(taps),
        second_kernel.reshape(taps),
        proj_bias.reshape(1, channels),
        first_bias.reshape(1, depth),
        second_bias.reshape(1, depth),
    )


def convolutions(
    projected, rows_dev, cols_dev, first_kernel, first_bias, second_kernel, second_bias
):
    grouped = projected.reshape(rows_dev, cols_dev, TILE_ROWS, TILE_COLS, 2, 2, CHANNELS)
    shuffled = jnp.transpose(grouped, (0, 2, 4, 1, 3, 5, 6)).reshape(
        rows_dev * TILE_ROWS * 2, cols_dev * TILE_COLS * 2, CHANNELS
    )
    activated = jax.nn.gelu(convolve(shuffled, first_kernel, first_bias)).astype(jnp.bfloat16)
    return convolve(activated, second_kernel, second_bias).astype(jnp.bfloat16)


def shards(
    query_window,
    key_window,
    value_window,
    query_index,
    key_index,
    proj_weight,
    proj_bias,
    first_kernel,
    first_bias,
    second_kernel,
    second_bias,
):
    rows_dev, cols_dev, tokens_win, features = query_window.shape
    flat = (rows_dev * cols_dev, tokens_win, features)
    owners = lax.axis_size("row") * lax.axis_size("col")
    fits = rows_dev == 1 and lax.axis_size("col") == 2 and owners == TILE_COLS
    fits = fits and tokens_win % (LINES * TILE_COLS) == 0 and tokens_win >= 4 * LINES * TILE_COLS
    if fits and cols_dev * LINES % 8 == 0 and features % LANES == 0:
        return fused(
            query_window.reshape(flat),
            key_window.reshape(flat),
            value_window.reshape(flat),
            query_index.reshape(flat),
            key_index.reshape(flat),
            proj_weight,
            proj_bias,
            first_kernel,
            first_bias,
            second_kernel,
            second_bias,
        )
    layout = (rows_dev * cols_dev, tokens_win, HEADS, HEAD_DIM)
    window_out = window_attend(
        query_window.reshape(layout), key_window.reshape(layout), value_window.reshape(layout)
    ).reshape(query_window.shape)
    count_row = lax.axis_size("row")
    count_col = lax.axis_size("col")
    owned_tokens = tokens_win // (count_row * count_col)
    moved = (
        lax.all_to_all(query_index, ("row", "col"), split_axis=2, concat_axis=0, tiled=True),
        lax.all_to_all(key_index, ("row", "col"), split_axis=2, concat_axis=0, tiled=True),
        lax.all_to_all(window_out, ("row", "col"), split_axis=2, concat_axis=0, tiled=True),
    )
    owner_shape = moved[0].shape
    across = (-1, owned_tokens, HEADS, HEAD_DIM)
    index_out = index_attend(
        moved[0].reshape(across), moved[1].reshape(across), moved[2].reshape(across)
    )
    index_rows = index_out.reshape(-1, features)
    owner_rows = (
        jnp.dot(index_rows, proj_weight, preferred_element_type=jnp.float32) + proj_bias
    ).astype(jnp.bfloat16)
    last = owner_rows.shape[-1]
    shaped = owner_rows.reshape(tuple(owner_shape[:-1]) + (last,))
    returned = lax.all_to_all(shaped, ("row", "col"), split_axis=0, concat_axis=2, tiled=True)
    projected = returned.reshape(rows_dev * cols_dev * tokens_win, last)
    return convolutions(
        projected, rows_dev, cols_dev, first_kernel, first_bias, second_kernel, second_bias
    )


def solution(mesh):
    in_specs = (
        P(("grp", "row"), "col", None, None),
        P(("grp", "row"), "col", None, None),
        P(("grp", "row"), "col", None, None),
        P(("grp", "row"), "col", None, None),
        P(("grp", "row"), "col", None, None),
        P(),
        P(),
        P(),
        P(),
        P(),
        P(),
    )
    out_specs = P(("grp", "row"), "col", None)
    return jax.shard_map(shards, mesh=mesh, in_specs=in_specs, out_specs=out_specs, check_vma=False)
```
